32 devices in a mesh: grp: 2 (over x), ctr: 16 (over z, y, core).
Axes of the slice: x: 2, y: 2, z: 4, core: 2. Of those that a mesh axis runs over, the one named last changes fastest.
Arguments:
- centres: bfloat16 [6144, 768], P(('grp', 'ctr')), parts along dimension 0
- sample_idx: int32 [1024], P(('grp', 'ctr')), parts along dimension 0, may hold values from 0 to 3071, as said below
- coef: float32 [6144], P(('grp', 'ctr')), parts along dimension 0
- metric_factor: bfloat16 [768, 768], replicated, may hold values from -0.21875 to 0.21875
Outputs:
- metric_new: float32 [1536, 768], P(('grp', 'ctr')), parts along dimension 0
- transformed: float32 [1024, 768], P(('grp', 'ctr')), parts along dimension 0
The draws below stay inside these ranges and needn't reach their ends.
There are 2 independent parts, one for each index of `grp`. The reference program is written for one: setup_inputs(seed, part) draws one part's arguments, and reference() takes and returns one part's arrays. A program takes and returns all parts, laid end to end along the dimension named above; an argument that names none is the same for every part. Nothing has to cross between parts.
Inputs may be any that keep to these rules, and one draw needn't show every extreme that they name: The 32 samples of the k-th aligned block of sample_idx are distinct centres of the k-th block of 192 centres.
All inputs are finite; a program needn't handle non-finite values.
Results may differ from the reference program's by a relative error of at most 0.0031.
Values may be sent and summed in bfloat16 or wider, within the bound.
A program may use at most 128 MiB of HBM per device.

```python
import jax
import jax.numpy as jnp
from jax import lax

D = 768
CTR_DEV = 192
S_DEV = 32
NC = 3072
S = 512
N_CTR = 16


def draw_centres(key, part):
    first, second = jax.random.split(key)
    base = jax.random.normal(first, (NC, D), jnp.float32)
    scales = jnp.exp(jax.random.uniform(second, (NC, 1), jnp.float32, 0.0, 2.3))
    return (base * scales).astype(jnp.bfloat16)


def draw_sample_idx(key, part):
    blocks = S // S_DEV
    scores = jax.random.randint(key, (blocks, CTR_DEV), 0, 2 ** 20) * CTR_DEV + jnp.arange(CTR_DEV)[None, :]
    order = jnp.argsort(scores, axis=1, stable=True)[:, :S_DEV]
    base = (jnp.arange(blocks) * CTR_DEV)[:, None]
    return (order + base).reshape(S).astype(jnp.int32)


def draw_coef(key, part):
    values = jax.random.normal(key, (NC,), jnp.float32)
    return values * (4000.0 / jnp.sqrt(jnp.float32(NC)))


def gaussian(stream_key, extent, deviation, bound, kind=jnp.bfloat16):
    array = deviation * jax.random.normal(stream_key, extent, jnp.float32)
    return jnp.clip(array, min=-bound, max=bound).astype(kind)


def setup_inputs(seed: int = 0, part: int = 0) -> dict:
    seeds = jax.random.split(jax.random.key(seed), 5)
    part_splits = jax.random.split(jax.random.fold_in(seeds[4], part), 5)
    centres = draw_centres(jax.random.fold_in(jax.random.fold_in(seeds[4], part), 71), part)
    sample_idx = draw_sample_idx(jax.random.fold_in(jax.random.fold_in(seeds[4], part), 71), part)
    coef = draw_coef(jax.random.fold_in(jax.random.fold_in(seeds[4], part), 71), part)
    metric_factor = gaussian(seeds[3], (D, D), D ** -0.5, 0.21875)
    return {"centres": centres, "sample_idx": sample_idx, "coef": coef, "metric_factor": metric_factor}


def block_grad(u_all, su, v_blk, coef_blk):
    width = u_all.shape[1]
    sv = lax.optimization_barrier(jnp.sum(v_blk.astype(jnp.float32) ** 2, axis=1))
    cross = jnp.dot(u_all, v_blk.T, preferred_element_type=jnp.float32)
    dist_sq = jnp.maximum(su[:, None] + sv[None, :] - 2.0 * cross, 0.0)
    radius = jnp.sqrt(dist_sq / width + 1.0)
    weight = coef_blk[None, :] * jnp.exp(-radius / 4.0) / (4.0 * width * radius)
    wround = weight.astype(jnp.bfloat16)
    return jnp.dot(wround, v_blk, preferred_element_type=jnp.float32) - lax.optimization_barrier(jnp.sum(weight, axis=1))[:, None] * u_all.astype(jnp.float32)

def reference(centres, sample_idx, coef, metric_factor):
    samples = jnp.take(centres, sample_idx.astype(jnp.int32), axis=0)
    u_all = jnp.dot(samples, metric_factor, preferred_element_type=jnp.float32).astype(jnp.bfloat16)
    su = lax.optimization_barrier(jnp.sum(u_all.astype(jnp.float32) ** 2, axis=1))
    v_all = jnp.dot(centres, metric_factor, preferred_element_type=jnp.float32).astype(jnp.bfloat16)
    v_blocks = v_all.reshape(N_CTR, CTR_DEV, D)
    c_blocks = coef.reshape(N_CTR, CTR_DEV)

    def step(total, pair):
        return (total + block_grad(u_all, su, pair[0], pair[1]), None)
    start = jnp.zeros((u_all.shape[0], D), jnp.float32)
    grad_u, _ = lax.scan(step, start, (v_blocks, c_blocks))
    factor = metric_factor.astype(jnp.float32)
    grads = jnp.dot(grad_u, factor.T, precision=lax.Precision.HIGHEST)
    agop = jnp.dot(grads.T, grads, precision=lax.Precision.HIGHEST) / u_all.shape[0]
    metric_new = agop * D / jnp.trace(agop)
    transformed = jnp.dot(grads, metric_new, precision=lax.Precision.HIGHEST)
    return (metric_new, transformed)
```

```python
import functools

import jax
import jax.numpy as jnp
from jax import lax
from jax.experimental import pallas as pl
from jax.experimental.pallas import tpu as pltpu
from jax.sharding import PartitionSpec as P

F32 = jnp.float32
BF16 = jnp.bfloat16
NT = (((1,), (1,)), ((), ()))


def halves(rows):
    return 2 if rows % 32 == 0 else 1


def parts(own):
    most = -(-own // 32) * 16
    cuts = []
    first = 0
    while first < own:
        count = min(most, own - first)
        cuts.append((first, count))
        first += count
    return cuts


def split(x):
    high = x.astype(BF16)
    return high, (x - high.astype(F32)).astype(BF16)


def flip(i, mask):
    out = i
    bit = 1
    while bit <= mask:
        if mask & bit:
            out = out + bit - 2 * bit * lax.rem(i // bit, 2)
        bit *= 2
    return out


def kernel(
    A, B, c_hbm, idx_hbm, coef_hbm, m_hbm, metric_ref, out_ref,
    c_ref, idx_ref, coef_ref, m_ref,
    cent, cfs, svs, ucol, acc, su_ref, wsum, psend, precv, gall,
    cs_send, cf_send, c_recv, cf_recv, u_send, u_recv, p_send, p_recv,
    g_send, g_recv, load,
):
    own, width = c_ref.shape
    rows = idx_ref.shape[1]
    cuts = parts(own)
    H = len(cuts)
    me = lax.axis_index("ctr")
    c = lax.rem(me, 2)
    b = lax.rem(me // 2, B)
    a = me // (2 * B)
    crossed = A == 4 and B == 2

    def dev(a_, b_, c_):
        return {"ctr": (a_ * B + b_) * 2 + c_}

    def at(mask):
        return {"ctr": flip(me, mask)}

    def copy(src, dst, ssem, rsem, to):
        return pltpu.make_async_remote_copy(
            src_ref=src, dst_ref=dst, send_sem=ssem, recv_sem=rsem,
            device_id=to, device_id_type=pl.DeviceIdType.MESH,
        )

    C, Y, Z = 1, 2, 2 * B
    partner = at(C)
    barrier = pltpu.get_barrier_semaphore()
    peers = [at(Z * k) for k in range(1, A)]
    peers += [at(Y * k) for k in range(1, B)]
    peers += [partner]
    if crossed:
        peers += [at(Z + Y)]
    for peer in peers:
        pl.semaphore_signal(barrier, inc=1, device_id=peer, device_id_type=pl.DeviceIdType.MESH)
    loads = [
        pltpu.make_async_copy(src, dst, load.at[k])
        for k, (src, dst) in enumerate(
            [(idx_hbm, idx_ref), (c_hbm, c_ref), (m_hbm, m_ref), (coef_hbm, coef_ref)]
        )
    ]
    for item in loads:
        item.start()
    pl.semaphore_wait(barrier, len(peers))

    sends = []

    def piece(ref, h):
        return ref.at[pl.ds(cuts[h][0], cuts[h][1])]

    for h in range(H):
        for k in range(1, B):
            sends.append(copy(
                piece(c_hbm, h), piece(cent.at[2 * k], h), cs_send.at[k * H + h],
                c_recv.at[2 * k * H + h], at(Y * k),
            ))
        if h == 0:
            for k in range(1, B):
                sends.append(
                    copy(coef_hbm, cfs.at[2 * k], cf_send.at[k], cf_recv.at[2 * k], at(Y * k))
                )
    sends.append(copy(coef_hbm, cfs.at[1], cf_send.at[0], cf_recv.at[1], partner))
    sends.append(copy(c_hbm, cent.at[1], cs_send.at[0], c_recv.at[H], partner))
    for s in sends:
        s.start()

    diag = lax.broadcasted_iota(jnp.int32, (rows, rows), 0) == lax.broadcasted_iota(
        jnp.int32, (rows, rows), 1
    )
    loads[0].wait()
    loads[1].wait()
    local_idx = (idx_ref[...] - me * own).astype(F32)
    column = jnp.sum(
        jnp.where(diag, jnp.broadcast_to(local_idx, (rows, rows)), 0.0), axis=1, keepdims=True
    )
    places = lax.broadcasted_iota(jnp.int32, (rows, own), 1).astype(F32)
    pick = jnp.where(places == column, 1.0, 0.0).astype(BF16)
    picked = jnp.dot(pick, c_ref[...], preferred_element_type=F32).astype(BF16)
    loads[2].wait()
    ucol[0] = jnp.dot(picked, m_ref[...], preferred_element_type=F32).astype(BF16)
    for k in reversed(range(1, A)):
        s = copy(ucol.at[0], ucol.at[k], u_send.at[k], u_recv.at[k], at(Z * k))
        s.start()
        sends.append(s)

    def coords(block):
        return jnp.dot(block, m_ref[...], preferred_element_type=F32).astype(BF16)

    def arrived(dst, rsem):
        copy(dst, dst, rsem, rsem, partner).wait_recv()

    def relay(k, h):
        j = 2 * k
        arrived(piece(cent.at[j], h), c_recv.at[j * H + h])
        first, count = cuts[h]
        cent[j, first : first + count] = coords(cent[j, first : first + count])
        hop = copy(
            piece(cent.at[j], h), piece(cent.at[j + 1], h),
            cs_send.at[(B - 1 + k) * H + h], c_recv.at[(j + 1) * H + h], partner,
        )
        hop.start()
        hops = [hop]
        if h == 0:
            arrived(cfs.at[j], cf_recv.at[j])
            hop = copy(
                cfs.at[j], cfs.at[j + 1], cf_send.at[B - 1 + k], cf_recv.at[j + 1], partner
            )
            hop.start()
            hops.append(hop)
        return hops

    def squared(v):
        vf = v.astype(F32)
        high, low = split(vf * vf)
        ones = jnp.ones((16, width), BF16)
        sums = lax.dot_general(ones, high, NT, preferred_element_type=F32) + lax.dot_general(
            ones, low, NT, preferred_element_type=F32
        )
        return sums[0:1]

    for slot, block in ((0, c_ref), (1, cent.at[1])):
        if slot:
            arrived(cent.at[1], c_recv.at[H])
        v = coords(block[...])
        cent[slot] = v
        svs[slot] = squared(v)
    early = relay(1, 0)
    for k in range(1, A):
        arrived(ucol.at[k], u_recv.at[k])
    uf = ucol[...].reshape(A * rows, width).astype(F32)
    su_ref[...] = jnp.sum(uf * uf, axis=1, keepdims=True)
    acc[...] = jnp.zeros_like(acc)
    wsum[...] = jnp.zeros_like(wsum)

    def add_block(v, coef_row, sv):
        u = ucol[...].reshape(A * rows, width)
        cross = lax.dot_general(u, v, NT, preferred_element_type=F32)
        dist_sq = jnp.maximum(su_ref[...] + sv - 2.0 * cross, 0.0)
        radius = jnp.sqrt(dist_sq / width + 1.0)
        weight = coef_row * jnp.exp(-radius / 4.0) / (4.0 * width * radius)
        acc[...] += jnp.dot(weight.astype(BF16), v, preferred_element_type=F32)
        wsum[...] += jnp.sum(weight, axis=1, keepdims=True)

    def add_pair(k, h):
        j = 2 * k
        if h == 0:
            arrived(cfs.at[j + 1], cf_recv.at[j + 1])
        arrived(piece(cent.at[j + 1], h), c_recv.at[(j + 1) * H + h])
        first, count = cuts[h]
        span = slice(first, first + count)
        v = jnp.concatenate([cent[j, span], cent[j + 1, span]], axis=0)
        coef_row = jnp.concatenate([cfs[j][:, span], cfs[j + 1][:, span]], axis=1)
        add_block(v, coef_row, squared(v))

    loads[3].wait()
    arrived(cfs.at[1], cf_recv.at[1])
    add_block(
        cent[0:2].reshape(2 * own, width),
        jnp.concatenate([coef_ref[...], cfs[1]], axis=1),
        jnp.concatenate([svs[0], svs[1]], axis=1),
    )

    def row_step(k, hops):
        for h in range(1, H):
            hops = hops + relay(k, h)
            add_pair(k, h - 1)
        add_pair(k, H - 1)
        return hops

    sends += row_step(1, early)

    def later_step(k, _):
        for hop in row_step(k, relay(k, 0)):
            hop.wait_send()
        return 0

    if B > 2:
        lax.fori_loop(2, B, later_step, 0)

    S = halves(rows)
    short = rows // S

    def settled(k, part):
        first = k * rows + part * short
        u = ucol[k, part * short : (part + 1) * short].astype(F32)
        return acc[first : first + short] - wsum[first : first + short] * u

    for part in range(S):
        span = pl.ds(part * short, short)
        for k in reversed(range(1, A)):
            psend[k, span] = settled(k, part).astype(BF16)
            s = copy(
                psend.at[k, span], precv.at[k, span], p_send.at[k * S + part],
                p_recv.at[k * S + part], at(Z * k),
            )
            s.start()
            sends.append(s)

    count = [0]

    def pass_on(part, slot, *masks):
        for mask in masks:
            s = copy(
                gall.at[part, slot], gall.at[part, slot ^ mask], g_send.at[count[0]],
                g_recv.at[part * n + (slot ^ mask)], at(mask),
            )
            count[0] += 1
            s.start()
            sends.append(s)

    def came(part, *slots):
        for slot in slots:
            arrived(gall.at[part, slot], g_recv.at[part * n + slot])

    def relayed(part, *slots):
        for slot in slots:
            came(part, slot)
            pass_on(part, slot, C)

    n = 2 * A * B
    samples = n * rows
    metric_rows = metric_ref.shape[0]
    padded = -(-metric_rows // 16) * 16
    own_grads = []
    for part in range(S):
        span = pl.ds(part * short, short)
        total = settled(0, part)
        for k in range(1, A):
            arrived(precv.at[k, span], p_recv.at[k * S + part])
            total += precv[k, span].astype(F32)
        high, low = split(total)
        both = lax.dot_general(
            jnp.concatenate([high, low], axis=0), m_ref[...], NT, preferred_element_type=F32
        )
        own_grads.append(both[:short] + both[short:])
        gall[part, 0] = own_grads[part].astype(BF16)
        if crossed:
            pass_on(part, 0, 2 * Z, Y, Z, Z + Y, C)
        else:
            pass_on(part, 0, *[Z * k for k in range(1, A)], *[Y * q for q in range(1, B)], C)

    grads = jnp.concatenate(own_grads, axis=0)
    largest = jnp.max(jnp.max(jnp.abs(grads), axis=1, keepdims=True), axis=0, keepdims=True)
    size = jnp.where(largest > 0.0, largest, 1.0) * 64.0
    line = lax.broadcasted_iota(jnp.int32, (padded, width), 0) + me * metric_rows
    choose = jnp.where(
        line == lax.broadcasted_iota(jnp.int32, (padded, width), 1), 1.0, 0.0
    ).astype(BF16)
    ghigh, glow = split(grads / size)
    left = jnp.concatenate([choose, ghigh, glow], axis=0)

    def gram(part, first, blocks):
        g = gall[part, first : first + blocks]
        full = g.reshape(blocks * short, width)
        inner = lax.dot_general(left, full, NT, preferred_element_type=F32)
        phigh, plow = split(inner[padded : padded + rows] + inner[padded + rows :])
        lhs = jnp.concatenate([inner[:padded].astype(BF16), phigh, plow], axis=0)
        gf = g.astype(F32)
        return [jnp.dot(lhs, full, preferred_element_type=F32), jnp.sum(gf * gf, axis=0)]

    grams = []
    if crossed:
        F = 2 * Z
        near = (Y, Z, Z + Y)
        for part in range(S):
            came(part, F)
            pass_on(part, F, Y, Z, Z + Y, C)
            relayed(part, *near)
        for part in range(S):
            came(part, C, *[slot + C for slot in near])
            grams.append(gram(part, 0, F))
            relayed(part, *[F + slot for slot in near])
        for part in range(S):
            came(part, F + C, *[F + slot + C for slot in near])
            grams.append(gram(part, F, F))
    else:
        for part in range(S):
            for k in range(A):
                if k:
                    came(part, Z * k)
                    pass_on(part, Z * k, *[Y * q for q in range(1, B)], C)
            for k in range(A):
                relayed(part, *[Z * k + Y * q for q in range(1, B)])
        for part in range(S):
            came(part, *range(C, n, 2))
            grams.append(gram(part, 0, n))

    result, squares = functools.reduce(lambda x, y: [x[0] + y[0], x[1] + y[1]], grams)
    trace = jnp.sum(
        jnp.sum(squares / samples, axis=1, keepdims=True), axis=0, keepdims=True
    )
    metric_ref[...] = (result[:metric_rows] / samples) * width / trace
    moved = result[padded : padded + rows] + result[padded + rows :]
    out_ref[...] = (moved / samples) * width / trace * size

    for s in sends:
        s.wait_send()


def finish(metric, moved, metric_ref, out_ref):
    metric_ref[...] = metric[...]
    out_ref[...] = moved[...]


def local(A, B, centres, sample_idx, coef, metric_factor):
    own, width = centres.shape
    rows = sample_idx.shape[0]
    n = A * B * 2
    dma = lambda k: pltpu.SemaphoreType.DMA((k,))
    vmem = pl.BlockSpec(memory_space=pltpu.VMEM)
    H = len(parts(own))
    S = halves(rows)
    limit = 60 * 2**20
    hbm = pl.BlockSpec(memory_space=pltpu.HBM)
    shapes = ((width // n, width), (rows, width))
    held = pl.pallas_call(
        functools.partial(kernel, A, B),
        out_shape=tuple(pltpu.VMEM(shape, F32) for shape in shapes),
        in_specs=[hbm] * 4,
        out_specs=(vmem, vmem),
        scratch_shapes=[
            pltpu.VMEM((own, width), BF16),
            pltpu.VMEM((1, rows), jnp.int32),
            pltpu.VMEM((1, own), F32),
            pltpu.VMEM((width, width), BF16),
            pltpu.VMEM((2 * B, own, width), BF16),
            pltpu.VMEM((2 * B, 1, own), F32),
            pltpu.VMEM((2 * B, 1, own), F32),
            pltpu.VMEM((A, rows, width), BF16),
            pltpu.VMEM((A * rows, width), F32),
            pltpu.VMEM((A * rows, 1), F32),
            pltpu.VMEM((A * rows, 1), F32),
            pltpu.VMEM((A, rows, width), BF16),
            pltpu.VMEM((A, rows, width), BF16),
            pltpu.VMEM((S, n, rows // S, width), BF16),
            dma(2 * B * H), dma(2 * B), dma(2 * B * H), dma(2 * B),
            dma(A), dma(A), dma(A * S), dma(A * S),
            dma((n + 16) * S), dma(n * S), dma(4),
        ],
        compiler_params=pltpu.CompilerParams(
            collective_id=0, has_side_effects=True, vmem_limit_bytes=limit
        ),
    )(centres, sample_idx.reshape(1, rows), coef.reshape(1, own), metric_factor)
    return pl.pallas_call(
        finish,
        out_shape=tuple(jax.ShapeDtypeStruct(shape, F32) for shape in shapes),
        in_specs=[vmem] * 2,
        out_specs=(vmem, vmem),
        compiler_params=pltpu.CompilerParams(vmem_limit_bytes=40 * 2**20),
    )(*held)


def solution(mesh):
    chips = mesh.shape["ctr"] // 2
    A = 1
    while A * A < chips:
        A *= 2
    B = chips // A
    placed = (P(("grp", "ctr"), None), P(("grp", "ctr")), P(("grp", "ctr")), P())
    return jax.shard_map(
        functools.partial(local, A, B),
        mesh=mesh,
        in_specs=placed,
        out_specs=(P(("grp", "ctr"), None), P(("grp", "ctr"), None)),
        check_vma=False,
    )
```

```python
import functools

import jax
import jax.numpy as jnp
from jax import lax
from jax.experimental import pallas as pl
from jax.experimental.pallas import tpu as pltpu
from jax.sharding import PartitionSpec as P

F32 = jnp.float32
BF16 = jnp.bfloat16
NT = (((1,), (1,)), ((), ()))


def halves(rows):
    return 2 if rows % 32 == 0 else 1


def parts(own):
    most = -(-own // 32) * 16
    cuts = []
    first = 0
    while first < own:
        count = min(most, own - first)
        cuts.append((first, count))
        first += count
    return cuts


def split(x):
    high = x.astype(BF16)
    return high, (x - high.astype(F32)).astype(BF16)


def flip(i, mask):
    out = i
    bit = 1
    while bit <= mask:
        if mask & bit:
            out = out + bit - 2 * bit * lax.rem(i // bit, 2)
        bit *= 2
    return out


def kernel(
    A, B, c_hbm, idx_hbm, coef_hbm, m_hbm, metric_ref, out_ref,
    c_ref, idx_ref, coef_ref, m_ref,
    cent, cfs, svs, ucol, acc, su_ref, wsum, psend, precv, gall,
    cs_send, cf_send, c_recv, cf_recv, u_send, u_recv, p_send, p_recv,
    g_send, g_recv, load, y_here, z_here,
):
    own, width = c_ref.shape
    rows = idx_ref.shape[1]
    cuts = parts(own)
    H = len(cuts)
    me = lax.axis_index("ctr")
    c = lax.rem(me, 2)
    b = lax.rem(me // 2, B)
    a = me // (2 * B)
    crossed = A == 4 and B == 2

    def dev(a_, b_, c_):
        return {"ctr": (a_ * B + b_) * 2 + c_}

    def at(mask):
        return {"ctr": flip(me, mask)}

    def copy(src, dst, ssem, rsem, to):
        return pltpu.make_async_remote_copy(
            src_ref=src, dst_ref=dst, send_sem=ssem, recv_sem=rsem,
            device_id=to, device_id_type=pl.DeviceIdType.MESH,
        )

    C, Y, Z = 1, 2, 2 * B
    partner = at(C)
    barrier = pltpu.get_barrier_semaphore()
    along_y = [Y * k for k in range(1, B)]
    along_z = [Z * k for k in range(1, A)] + ([Z + Y] if crossed else [])

    def signal(sem, to):
        pl.semaphore_signal(sem, inc=1, device_id=to, device_id_type=pl.DeviceIdType.MESH)

    def chip(mask, core):
        return {"ctr": flip(me, mask) - c + core}

    @pl.when(c == 1)
    def _():
        signal(barrier, chip(0, 0))

    for mask in along_y:
        signal(barrier, chip(mask, 0))
    for mask in along_z:
        signal(barrier, chip(mask, 1))
    loads = [
        pltpu.make_async_copy(src, dst, load.at[k])
        for k, (src, dst) in enumerate(
            [(idx_hbm, idx_ref), (c_hbm, c_ref), (m_hbm, m_ref), (coef_hbm, coef_ref)]
        )
    ]
    for item in loads:
        item.start()

    @pl.when(c == 0)
    def _():
        pl.semaphore_wait(barrier, 1 + 2 * len(along_y))
        signal(y_here, partner)

    @pl.when(c == 1)
    def _():
        pl.semaphore_wait(y_here, 1)

    sends = []

    def piece(ref, h):
        return ref.at[pl.ds(cuts[h][0], cuts[h][1])]

    for h in range(H):
        for k in range(1, B):
            sends.append(copy(
                piece(c_hbm, h), piece(cent.at[2 * k], h), cs_send.at[k * H + h],
                c_recv.at[2 * k * H + h], at(Y * k),
            ))
        if h == 0:
            for k in range(1, B):
                sends.append(
                    copy(coef_hbm, cfs.at[2 * k], cf_send.at[k], cf_recv.at[2 * k], at(Y * k))
                )
    sends.append(copy(coef_hbm, cfs.at[1], cf_send.at[0], cf_recv.at[1], partner))
    sends.append(copy(c_hbm, cent.at[1], cs_send.at[0], c_recv.at[H], partner))
    for s in sends:
        s.start()

    diag = lax.broadcasted_iota(jnp.int32, (rows, rows), 0) == lax.broadcasted_iota(
        jnp.int32, (rows, rows), 1
    )
    loads[0].wait()
    loads[1].wait()
    local_idx = (idx_ref[...] - me * own).astype(F32)
    column = jnp.sum(
        jnp.where(diag, jnp.broadcast_to(local_idx, (rows, rows)), 0.0), axis=1, keepdims=True
    )
    places = lax.broadcasted_iota(jnp.int32, (rows, own), 1).astype(F32)
    pick = jnp.where(places == column, 1.0, 0.0).astype(BF16)
    picked = jnp.dot(pick, c_ref[...], preferred_element_type=F32).astype(BF16)
    loads[2].wait()
    ucol[0] = jnp.dot(picked, m_ref[...], preferred_element_type=F32).astype(BF16)

    def coords(block):
        return jnp.dot(block, m_ref[...], preferred_element_type=F32).astype(BF16)

    def arrived(dst, rsem):
        copy(dst, dst, rsem, rsem, partner).wait_recv()

    def relay(k, h):
        j = 2 * k
        arrived(piece(cent.at[j], h), c_recv.at[j * H + h])
        first, count = cuts[h]
        cent[j, first : first + count] = coords(cent[j, first : first + count])
        hop = copy(
            piece(cent.at[j], h), piece(cent.at[j + 1], h),
            cs_send.at[(B - 1 + k) * H + h], c_recv.at[(j + 1) * H + h], partner,
        )
        hop.start()
        hops = [hop]
        if h == 0:
            arrived(cfs.at[j], cf_recv.at[j])
            hop = copy(
                cfs.at[j], cfs.at[j + 1], cf_send.at[B - 1 + k], cf_recv.at[j + 1], partner
            )
            hop.start()
            hops.append(hop)
        return hops

    def squared(v):
        vf = v.astype(F32)
        high, low = split(vf * vf)
        ones = jnp.ones((16, width), BF16)
        sums = lax.dot_general(ones, high, NT, preferred_element_type=F32) + lax.dot_general(
            ones, low, NT, preferred_element_type=F32
        )
        return sums[0:1]

    def ready(slot, block):
        v = coords(block)
        cent[slot] = v
        svs[slot] = squared(v)

    ready(0, c_ref[...])

    @pl.when(c == 1)
    def _():
        pl.semaphore_wait(barrier, 2 * len(along_z))
        signal(z_here, partner)

    @pl.when(c == 0)
    def _():
        pl.semaphore_wait(z_here, 1)

    for k in reversed(range(1, A)):
        s = copy(ucol.at[0], ucol.at[k], u_send.at[k], u_recv.at[k], at(Z * k))
        s.start()
        sends.append(s)
    arrived(cent.at[1], c_recv.at[H])
    ready(1, cent[1])
    early = relay(1, 0)
    for k in range(1, A):
        arrived(ucol.at[k], u_recv.at[k])
    uf = ucol[...].reshape(A * rows, width).astype(F32)
    su_ref[...] = jnp.sum(uf * uf, axis=1, keepdims=True)
    acc[...] = jnp.zeros_like(acc)
    wsum[...] = jnp.zeros_like(wsum)

    def add_block(v, coef_row, sv):
        u = ucol[...].reshape(A * rows, width)
        cross = lax.dot_general(u, v, NT, preferred_element_type=F32)
        dist_sq = jnp.maximum(su_ref[...] + sv - 2.0 * cross, 0.0)
        radius = jnp.sqrt(dist_sq / width + 1.0)
        weight = coef_row * jnp.exp(-radius / 4.0) / (4.0 * width * radius)
        acc[...] += jnp.dot(weight.astype(BF16), v, preferred_element_type=F32)
        wsum[...] += jnp.sum(weight, axis=1, keepdims=True)

    def add_pair(k, h):
        j = 2 * k
        if h == 0:
            arrived(cfs.at[j + 1], cf_recv.at[j + 1])
        arrived(piece(cent.at[j + 1], h), c_recv.at[(j + 1) * H + h])
        first, count = cuts[h]
        span = slice(first, first + count)
        v = jnp.concatenate([cent[j, span], cent[j + 1, span]], axis=0)
        coef_row = jnp.concatenate([cfs[j][:, span], cfs[j + 1][:, span]], axis=1)
        add_block(v, coef_row, squared(v))

    loads[3].wait()
    arrived(cfs.at[1], cf_recv.at[1])
    add_block(
        cent[0:2].reshape(2 * own, width),
        jnp.concatenate([coef_ref[...], cfs[1]], axis=1),
        jnp.concatenate([svs[0], svs[1]], axis=1),
    )

    def row_step(k, hops):
        for h in range(1, H):
            hops = hops + relay(k, h)
            add_pair(k, h - 1)
        add_pair(k, H - 1)
        return hops

    sends += row_step(1, early)

    def later_step(k, _):
        for hop in row_step(k, relay(k, 0)):
            hop.wait_send()
        return 0

    if B > 2:
        lax.fori_loop(2, B, later_step, 0)

    S = halves(rows)
    short = rows // S

    def settled(k, part):
        first = k * rows + part * short
        u = ucol[k, part * short : (part + 1) * short].astype(F32)
        return acc[first : first + short] - wsum[first : first + short] * u

    for part in range(S):
        span = pl.ds(part * short, short)
        for k in reversed(range(1, A)):
            psend[k, span] = settled(k, part).astype(BF16)
            s = copy(
                psend.at[k, span], precv.at[k, span], p_send.at[k * S + part],
                p_recv.at[k * S + part], at(Z * k),
            )
            s.start()
            sends.append(s)

    count = [0]

    def pass_on(part, slot, *masks):
        for mask in masks:
            s = copy(
                gall.at[part, slot], gall.at[part, slot ^ mask], g_send.at[count[0]],
                g_recv.at[part * n + (slot ^ mask)], at(mask),
            )
            count[0] += 1
            s.start()
            sends.append(s)

    def came(part, *slots):
        for slot in slots:
            arrived(gall.at[part, slot], g_recv.at[part * n + slot])

    def relayed(part, *slots):
        for slot in slots:
            came(part, slot)
            pass_on(part, slot, C)

    n = 2 * A * B
    samples = n * rows
    metric_rows = metric_ref.shape[0]
    padded = -(-metric_rows // 16) * 16
    own_grads = []
    for part in range(S):
        span = pl.ds(part * short, short)
        total = settled(0, part)
        for k in range(1, A):
            arrived(precv.at[k, span], p_recv.at[k * S + part])
            total += precv[k, span].astype(F32)
        high, low = split(total)
        both = lax.dot_general(
            jnp.concatenate([high, low], axis=0), m_ref[...], NT, preferred_element_type=F32
        )
        own_grads.append(both[:short] + both[short:])
        gall[part, 0] = own_grads[part].astype(BF16)
        if crossed:
            pass_on(part, 0, 2 * Z, Y, Z, Z + Y, C)
        else:
            pass_on(part, 0, *[Z * k for k in range(1, A)], *[Y * q for q in range(1, B)], C)

    grads = jnp.concatenate(own_grads, axis=0)
    largest = jnp.max(jnp.max(jnp.abs(grads), axis=1, keepdims=True), axis=0, keepdims=True)
    size = jnp.where(largest > 0.0, largest, 1.0) * 64.0
    line = lax.broadcasted_iota(jnp.int32, (padded, width), 0) + me * metric_rows
    choose = jnp.where(
        line == lax.broadcasted_iota(jnp.int32, (padded, width), 1), 1.0, 0.0
    ).astype(BF16)
    ghigh, glow = split(grads / size)
    left = jnp.concatenate([choose, ghigh, glow], axis=0)

    def gram(part, first, blocks):
        g = gall[part, first : first + blocks]
        full = g.reshape(blocks * short, width)
        inner = lax.dot_general(left, full, NT, preferred_element_type=F32)
        phigh, plow = split(inner[padded : padded + rows] + inner[padded + rows :])
        lhs = jnp.concatenate([inner[:padded].astype(BF16), phigh, plow], axis=0)
        gf = g.astype(F32)
        return [jnp.dot(lhs, full, preferred_element_type=F32), jnp.sum(gf * gf, axis=0)]

    grams = []
    if crossed:
        F = 2 * Z
        near = (Y, Z, Z + Y)
        for part in range(S):
            came(part, F)
            pass_on(part, F, Y, Z, Z + Y, C)
            relayed(part, *near)
        for part in range(S):
            came(part, C, *[slot + C for slot in near])
            grams.append(gram(part, 0, F))
            relayed(part, *[F + slot for slot in near])
        for part in range(S):
            came(part, F + C, *[F + slot + C for slot in near])
            grams.append(gram(part, F, F))
    else:
        for part in range(S):
            for k in range(A):
                if k:
                    came(part, Z * k)
                    pass_on(part, Z * k, *[Y * q for q in range(1, B)], C)
            for k in range(A):
                relayed(part, *[Z * k + Y * q for q in range(1, B)])
        for part in range(S):
            came(part, *range(C, n, 2))
            grams.append(gram(part, 0, n))

    result, squares = functools.reduce(lambda x, y: [x[0] + y[0], x[1] + y[1]], grams)
    trace = jnp.sum(
        jnp.sum(squares / samples, axis=1, keepdims=True), axis=0, keepdims=True
    )
    metric_ref[...] = (result[:metric_rows] / samples) * width / trace
    moved = result[padded : padded + rows] + result[padded + rows :]
    out_ref[...] = (moved / samples) * width / trace * size

    for s in sends:
        s.wait_send()


def finish(metric, moved, metric_ref, out_ref):
    metric_ref[...] = metric[...]
    out_ref[...] = moved[...]


def local(A, B, centres, sample_idx, coef, metric_factor):
    own, width = centres.shape
    rows = sample_idx.shape[0]
    n = A * B * 2
    dma = lambda k: pltpu.SemaphoreType.DMA((k,))
    vmem = pl.BlockSpec(memory_space=pltpu.VMEM)
    H = len(parts(own))
    S = halves(rows)
    limit = 60 * 2**20
    hbm = pl.BlockSpec(memory_space=pltpu.HBM)
    shapes = ((width // n, width), (rows, width))
    held = pl.pallas_call(
        functools.partial(kernel, A, B),
        out_shape=tuple(pltpu.VMEM(shape, F32) for shape in shapes),
        in_specs=[hbm] * 4,
        out_specs=(vmem, vmem),
        scratch_shapes=[
            pltpu.VMEM((own, width), BF16),
            pltpu.VMEM((1, rows), jnp.int32),
            pltpu.VMEM((1, own), F32),
            pltpu.VMEM((width, width), BF16),
            pltpu.VMEM((2 * B, own, width), BF16),
            pltpu.VMEM((2 * B, 1, own), F32),
            pltpu.VMEM((2 * B, 1, own), F32),
            pltpu.VMEM((A, rows, width), BF16),
            pltpu.VMEM((A * rows, width), F32),
            pltpu.VMEM((A * rows, 1), F32),
            pltpu.VMEM((A * rows, 1), F32),
            pltpu.VMEM((A, rows, width), BF16),
            pltpu.VMEM((A, rows, width), BF16),
            pltpu.VMEM((S, n, rows // S, width), BF16),
            dma(2 * B * H), dma(2 * B), dma(2 * B * H), dma(2 * B),
            dma(A), dma(A), dma(A * S), dma(A * S),
            dma((n + 16) * S), dma(n * S), dma(4),
            pltpu.SemaphoreType.REGULAR, pltpu.SemaphoreType.REGULAR,
        ],
        compiler_params=pltpu.CompilerParams(
            collective_id=0, has_side_effects=True, vmem_limit_bytes=limit
        ),
    )(centres, sample_idx.reshape(1, rows), coef.reshape(1, own), metric_factor)
    return pl.pallas_call(
        finish,
        out_shape=tuple(jax.ShapeDtypeStruct(shape, F32) for shape in shapes),
        in_specs=[vmem] * 2,
        out_specs=(vmem, vmem),
        compiler_params=pltpu.CompilerParams(vmem_limit_bytes=40 * 2**20),
    )(*held)


def solution(mesh):
    chips = mesh.shape["ctr"] // 2
    A = 1
    while A * A < chips:
        A *= 2
    B = chips // A
    placed = (P(("grp", "ctr"), None), P(("grp", "ctr")), P(("grp", "ctr")), P())
    return jax.shard_map(
        functools.partial(local, A, B),
        mesh=mesh,
        in_specs=placed,
        out_specs=(P(("grp", "ctr"), None), P(("grp", "ctr"), None)),
        check_vma=False,
    )
```

```python
import functools

import jax
import jax.numpy as jnp
from jax import lax
from jax.experimental import pallas as pl
from jax.experimental.pallas import tpu as pltpu
from jax.sharding import PartitionSpec as P

F32 = jnp.float32
BF16 = jnp.bfloat16
NT = (((1,), (1,)), ((), ()))


def halves(rows):
    return 2 if rows % 32 == 0 else 1


def parts(own):
    most = -(-own // 32) * 16
    cuts = []
    first = 0
    while first < own:
        count = min(most, own - first)
        cuts.append((first, count))
        first += count
    return cuts


def split(x):
    high = x.astype(BF16)
    return high, (x - high.astype(F32)).astype(BF16)


def flip(i, mask):
    out = i
    bit = 1
    while bit <= mask:
        if mask & bit:
            out = out + bit - 2 * bit * lax.rem(i // bit, 2)
        bit *= 2
    return out


def kernel(
    A, B, c_hbm, idx_hbm, coef_hbm, m_hbm, metric_ref, out_ref,
    c_ref, idx_ref, coef_ref, m_ref,
    cent, cfs, svs, ucol, acc, su_ref, wsum, psend, precv, gall,
    cs_send, cf_send, c_recv, cf_recv, u_send, u_recv, p_send, p_recv,
    g_send, g_recv, load, z_here,
):
    own, width = c_ref.shape
    rows = idx_ref.shape[1]
    cuts = parts(own)
    H = len(cuts)
    me = lax.axis_index("ctr")
    c = lax.rem(me, 2)
    b = lax.rem(me // 2, B)
    a = me // (2 * B)
    crossed = A == 4 and B == 2

    def dev(a_, b_, c_):
        return {"ctr": (a_ * B + b_) * 2 + c_}

    def at(mask):
        return {"ctr": flip(me, mask)}

    def copy(src, dst, ssem, rsem, to):
        return pltpu.make_async_remote_copy(
            src_ref=src, dst_ref=dst, send_sem=ssem, recv_sem=rsem,
            device_id=to, device_id_type=pl.DeviceIdType.MESH,
        )

    C, Y, Z = 1, 2, 2 * B
    partner = at(C)
    barrier = pltpu.get_barrier_semaphore()
    along_z = [Z * k for k in range(1, A)] + ([Z + Y] if crossed else [])

    def signal(sem, to):
        pl.semaphore_signal(sem, inc=1, device_id=to, device_id_type=pl.DeviceIdType.MESH)

    def higher(mask):
        top = 1
        while 2 * top <= mask // Z:
            top *= 2
        return lax.rem(a // top, 2)

    for mask in [Y * k for k in range(1, B)] + [C]:
        signal(barrier, at(mask))
    for mask in along_z:
        @pl.when(higher(mask) == 0)
        def _():
            signal(barrier, at(mask))
    loads = [
        pltpu.make_async_copy(src, dst, load.at[k])
        for k, (src, dst) in enumerate(
            [(idx_hbm, idx_ref), (c_hbm, c_ref), (m_hbm, m_ref), (coef_hbm, coef_ref)]
        )
    ]
    for item in loads:
        item.start()
    pl.semaphore_wait(barrier, B + sum(higher(mask) for mask in along_z))

    sends = []

    def piece(ref, h):
        return ref.at[pl.ds(cuts[h][0], cuts[h][1])]

    for h in range(H):
        for k in range(1, B):
            sends.append(copy(
                piece(c_hbm, h), piece(cent.at[2 * k], h), cs_send.at[k * H + h],
                c_recv.at[2 * k * H + h], at(Y * k),
            ))
        if h == 0:
            for k in range(1, B):
                sends.append(
                    copy(coef_hbm, cfs.at[2 * k], cf_send.at[k], cf_recv.at[2 * k], at(Y * k))
                )
    sends.append(copy(coef_hbm, cfs.at[1], cf_send.at[0], cf_recv.at[1], partner))
    sends.append(copy(c_hbm, cent.at[1], cs_send.at[0], c_recv.at[H], partner))
    for s in sends:
        s.start()
    for i, mask in enumerate(along_z):
        @pl.when(higher(mask) == 1)
        def _():
            signal(z_here.at[i], at(mask))

    diag = lax.broadcasted_iota(jnp.int32, (rows, rows), 0) == lax.broadcasted_iota(
        jnp.int32, (rows, rows), 1
    )
    loads[0].wait()
    loads[1].wait()
    local_idx = (idx_ref[...] - me * own).astype(F32)
    column = jnp.sum(
        jnp.where(diag, jnp.broadcast_to(local_idx, (rows, rows)), 0.0), axis=1, keepdims=True
    )
    places = lax.broadcasted_iota(jnp.int32, (rows, own), 1).astype(F32)
    pick = jnp.where(places == column, 1.0, 0.0).astype(BF16)
    picked = jnp.dot(pick, c_ref[...], preferred_element_type=F32).astype(BF16)
    loads[2].wait()
    ucol[0] = jnp.dot(picked, m_ref[...], preferred_element_type=F32).astype(BF16)
    to_row = [
        copy(ucol.at[0], ucol.at[k], u_send.at[k], u_recv.at[k], at(Z * k)) for k in range(1, A)
    ]
    sends += to_row
    for i, mask in reversed(list(enumerate(along_z[: A - 1]))):
        @pl.when(higher(mask) == 1)
        def _():
            to_row[i].start()

    def coords(block):
        return jnp.dot(block, m_ref[...], preferred_element_type=F32).astype(BF16)

    def arrived(dst, rsem):
        copy(dst, dst, rsem, rsem, partner).wait_recv()

    def relay(k, h):
        j = 2 * k
        arrived(piece(cent.at[j], h), c_recv.at[j * H + h])
        first, count = cuts[h]
        cent[j, first : first + count] = coords(cent[j, first : first + count])
        hop = copy(
            piece(cent.at[j], h), piece(cent.at[j + 1], h),
            cs_send.at[(B - 1 + k) * H + h], c_recv.at[(j + 1) * H + h], partner,
        )
        hop.start()
        hops = [hop]
        if h == 0:
            arrived(cfs.at[j], cf_recv.at[j])
            hop = copy(
                cfs.at[j], cfs.at[j + 1], cf_send.at[B - 1 + k], cf_recv.at[j + 1], partner
            )
            hop.start()
            hops.append(hop)
        return hops

    def squared(v):
        vf = v.astype(F32)
        high, low = split(vf * vf)
        ones = jnp.ones((16, width), BF16)
        sums = lax.dot_general(ones, high, NT, preferred_element_type=F32) + lax.dot_general(
            ones, low, NT, preferred_element_type=F32
        )
        return sums[0:1]

    def ready(slot, block):
        v = coords(block)
        cent[slot] = v
        svs[slot] = squared(v)

    ready(0, c_ref[...])

    for i, mask in enumerate(along_z):
        @pl.when(higher(mask) == 0)
        def _():
            pl.semaphore_wait(z_here.at[i], 1)
            if i < A - 1:
                to_row[i].start()

    arrived(cent.at[1], c_recv.at[H])
    ready(1, cent[1])
    early = relay(1, 0)
    for k in range(1, A):
        arrived(ucol.at[k], u_recv.at[k])
    uf = ucol[...].reshape(A * rows, width).astype(F32)
    su_ref[...] = jnp.sum(uf * uf, axis=1, keepdims=True)
    acc[...] = jnp.zeros_like(acc)
    wsum[...] = jnp.zeros_like(wsum)

    def add_block(v, coef_row, sv):
        u = ucol[...].reshape(A * rows, width)
        cross = lax.dot_general(u, v, NT, preferred_element_type=F32)
        dist_sq = jnp.maximum(su_ref[...] + sv - 2.0 * cross, 0.0)
        radius = jnp.sqrt(dist_sq / width + 1.0)
        weight = coef_row * jnp.exp(-radius / 4.0) / (4.0 * width * radius)
        acc[...] += jnp.dot(weight.astype(BF16), v, preferred_element_type=F32)
        wsum[...] += jnp.sum(weight, axis=1, keepdims=True)

    def add_pair(k, h):
        j = 2 * k
        if h == 0:
            arrived(cfs.at[j + 1], cf_recv.at[j + 1])
        arrived(piece(cent.at[j + 1], h), c_recv.at[(j + 1) * H + h])
        first, count = cuts[h]
        span = slice(first, first + count)
        v = jnp.concatenate([cent[j, span], cent[j + 1, span]], axis=0)
        coef_row = jnp.concatenate([cfs[j][:, span], cfs[j + 1][:, span]], axis=1)
        add_block(v, coef_row, squared(v))

    loads[3].wait()
    arrived(cfs.at[1], cf_recv.at[1])
    add_block(
        cent[0:2].reshape(2 * own, width),
        jnp.concatenate([coef_ref[...], cfs[1]], axis=1),
        jnp.concatenate([svs[0], svs[1]], axis=1),
    )

    def row_step(k, hops):
        for h in range(1, H):
            hops = hops + relay(k, h)
            add_pair(k, h - 1)
        add_pair(k, H - 1)
        return hops

    sends += row_step(1, early)

    def later_step(k, _):
        for hop in row_step(k, relay(k, 0)):
            hop.wait_send()
        return 0

    if B > 2:
        lax.fori_loop(2, B, later_step, 0)

    S = halves(rows)
    short = rows // S

    def settled(k, part):
        first = k * rows + part * short
        u = ucol[k, part * short : (part + 1) * short].astype(F32)
        return acc[first : first + short] - wsum[first : first + short] * u

    for part in range(S):
        span = pl.ds(part * short, short)
        for k in reversed(range(1, A)):
            psend[k, span] = settled(k, part).astype(BF16)
            s = copy(
                psend.at[k, span], precv.at[k, span], p_send.at[k * S + part],
                p_recv.at[k * S + part], at(Z * k),
            )
            s.start()
            sends.append(s)

    count = [0]

    def pass_on(part, slot, *masks):
        for mask in masks:
            s = copy(
                gall.at[part, slot], gall.at[part, slot ^ mask], g_send.at[count[0]],
                g_recv.at[part * n + (slot ^ mask)], at(mask),
            )
            count[0] += 1
            s.start()
            sends.append(s)

    def came(part, *slots):
        for slot in slots:
            arrived(gall.at[part, slot], g_recv.at[part * n + slot])

    def relayed(part, *slots):
        for slot in slots:
            came(part, slot)
            pass_on(part, slot, C)

    n = 2 * A * B
    samples = n * rows
    metric_rows = metric_ref.shape[0]
    padded = -(-metric_rows // 16) * 16
    own_grads = []
    for part in range(S):
        span = pl.ds(part * short, short)
        total = settled(0, part)
        for k in range(1, A):
            arrived(precv.at[k, span], p_recv.at[k * S + part])
            total += precv[k, span].astype(F32)
        high, low = split(total)
        both = lax.dot_general(
            jnp.concatenate([high, low], axis=0), m_ref[...], NT, preferred_element_type=F32
        )
        own_grads.append(both[:short] + both[short:])
        gall[part, 0] = own_grads[part].astype(BF16)
        if crossed:
            pass_on(part, 0, 2 * Z, Y, Z, Z + Y, C)
        else:
            pass_on(part, 0, *[Z * k for k in range(1, A)], *[Y * q for q in range(1, B)], C)

    grads = jnp.concatenate(own_grads, axis=0)
    largest = jnp.max(jnp.max(jnp.abs(grads), axis=1, keepdims=True), axis=0, keepdims=True)
    size = jnp.where(largest > 0.0, largest, 1.0) * 64.0
    line = lax.broadcasted_iota(jnp.int32, (padded, width), 0) + me * metric_rows
    choose = jnp.where(
        line == lax.broadcasted_iota(jnp.int32, (padded, width), 1), 1.0, 0.0
    ).astype(BF16)
    ghigh, glow = split(grads / size)
    left = jnp.concatenate([choose, ghigh, glow], axis=0)

    def gram(part, first, blocks):
        g = gall[part, first : first + blocks]
        full = g.reshape(blocks * short, width)
        inner = lax.dot_general(left, full, NT, preferred_element_type=F32)
        phigh, plow = split(inner[padded : padded + rows] + inner[padded + rows :])
        lhs = jnp.concatenate([inner[:padded].astype(BF16), phigh, plow], axis=0)
        gf = g.astype(F32)
        return [jnp.dot(lhs, full, preferred_element_type=F32), jnp.sum(gf * gf, axis=0)]

    grams = []
    if crossed:
        F = 2 * Z
        near = (Y, Z, Z + Y)
        for part in range(S):
            came(part, F)
            pass_on(part, F, Y, Z, Z + Y, C)
            relayed(part, *near)
        for part in range(S):
            came(part, C, *[slot + C for slot in near])
            grams.append(gram(part, 0, F))
            relayed(part, *[F + slot for slot in near])
        for part in range(S):
            came(part, F + C, *[F + slot + C for slot in near])
            grams.append(gram(part, F, F))
    else:
        for part in range(S):
            for k in range(A):
                if k:
                    came(part, Z * k)
                    pass_on(part, Z * k, *[Y * q for q in range(1, B)], C)
            for k in range(A):
                relayed(part, *[Z * k + Y * q for q in range(1, B)])
        for part in range(S):
            came(part, *range(C, n, 2))
            grams.append(gram(part, 0, n))

    result, squares = functools.reduce(lambda x, y: [x[0] + y[0], x[1] + y[1]], grams)
    trace = jnp.sum(
        jnp.sum(squares / samples, axis=1, keepdims=True), axis=0, keepdims=True
    )
    metric_ref[...] = (result[:metric_rows] / samples) * width / trace
    moved = result[padded : padded + rows] + result[padded + rows :]
    out_ref[...] = (moved / samples) * width / trace * size

    for s in sends:
        s.wait_send()


def finish(metric, moved, metric_ref, out_ref):
    metric_ref[...] = metric[...]
    out_ref[...] = moved[...]


def local(A, B, centres, sample_idx, coef, metric_factor):
    own, width = centres.shape
    rows = sample_idx.shape[0]
    n = A * B * 2
    dma = lambda k: pltpu.SemaphoreType.DMA((k,))
    vmem = pl.BlockSpec(memory_space=pltpu.VMEM)
    H = len(parts(own))
    S = halves(rows)
    limit = 60 * 2**20
    hbm = pl.BlockSpec(memory_space=pltpu.HBM)
    shapes = ((width // n, width), (rows, width))
    held = pl.pallas_call(
        functools.partial(kernel, A, B),
        out_shape=tuple(pltpu.VMEM(shape, F32) for shape in shapes),
        in_specs=[hbm] * 4,
        out_specs=(vmem, vmem),
        scratch_shapes=[
            pltpu.VMEM((own, width), BF16),
            pltpu.VMEM((1, rows), jnp.int32),
            pltpu.VMEM((1, own), F32),
            pltpu.VMEM((width, width), BF16),
            pltpu.VMEM((2 * B, own, width), BF16),
            pltpu.VMEM((2 * B, 1, own), F32),
            pltpu.VMEM((2 * B, 1, own), F32),
            pltpu.VMEM((A, rows, width), BF16),
            pltpu.VMEM((A * rows, width), F32),
            pltpu.VMEM((A * rows, 1), F32),
            pltpu.VMEM((A * rows, 1), F32),
            pltpu.VMEM((A, rows, width), BF16),
            pltpu.VMEM((A, rows, width), BF16),
            pltpu.VMEM((S, n, rows // S, width), BF16),
            dma(2 * B * H), dma(2 * B), dma(2 * B * H), dma(2 * B),
            dma(A), dma(A), dma(A * S), dma(A * S),
            dma((n + 16) * S), dma(n * S), dma(4),
            pltpu.SemaphoreType.REGULAR((A,)),
        ],
        compiler_params=pltpu.CompilerParams(
            collective_id=0, has_side_effects=True, vmem_limit_bytes=limit
        ),
    )(centres, sample_idx.reshape(1, rows), coef.reshape(1, own), metric_factor)
    return pl.pallas_call(
        finish,
        out_shape=tuple(jax.ShapeDtypeStruct(shape, F32) for shape in shapes),
        in_specs=[vmem] * 2,
        out_specs=(vmem, vmem),
        compiler_params=pltpu.CompilerParams(vmem_limit_bytes=40 * 2**20),
    )(*held)


def solution(mesh):
    chips = mesh.shape["ctr"] // 2
    A = 1
    while A * A < chips:
        A *= 2
    B = chips // A
    placed = (P(("grp", "ctr"), None), P(("grp", "ctr")), P(("grp", "ctr")), P())
    return jax.shard_map(
        functools.partial(local, A, B),
        mesh=mesh,
        in_specs=placed,
        out_specs=(P(("grp", "ctr"), None), P(("grp", "ctr"), None)),
        check_vma=False,
    )
```

```python
import functools

import jax
import jax.numpy as jnp
from jax import lax
from jax.experimental import pallas as pl
from jax.experimental.pallas import tpu as pltpu
from jax.sharding import PartitionSpec as P

F32 = jnp.float32
BF16 = jnp.bfloat16
NT = (((1,), (1,)), ((), ()))


def halves(rows):
    return 2 if rows % 32 == 0 else 1


def parts(own):
    most = -(-own // 32) * 16
    cuts = []
    first = 0
    while first < own:
        count = min(most, own - first)
        cuts.append((first, count))
        first += count
    return cuts


def split(x):
    high = x.astype(BF16)
    return high, (x - high.astype(F32)).astype(BF16)


def flip(i, mask):
    out = i
    bit = 1
    while bit <= mask:
        if mask & bit:
            out = out + bit - 2 * bit * lax.rem(i // bit, 2)
        bit *= 2
    return out


def kernel(
    A, B, c_hbm, idx_hbm, coef_hbm, m_hbm, metric_ref, out_ref,
    c_ref, idx_ref, coef_ref, m_ref,
    cent, cfs, svs, ucol, acc, su_ref, wsum, psend, precv, gall,
    cs_send, cf_send, c_recv, cf_recv, u_send, u_recv, p_send, p_recv,
    g_send, g_recv, load, z_here,
):
    own, width = c_ref.shape
    rows = idx_ref.shape[1]
    cuts = parts(own)
    H = len(cuts)
    me = lax.axis_index("ctr")
    c = lax.rem(me, 2)
    b = lax.rem(me // 2, B)
    a = me // (2 * B)
    crossed = A == 4 and B == 2

    def dev(a_, b_, c_):
        return {"ctr": (a_ * B + b_) * 2 + c_}

    def at(mask):
        return {"ctr": flip(me, mask)}

    def copy(src, dst, ssem, rsem, to):
        return pltpu.make_async_remote_copy(
            src_ref=src, dst_ref=dst, send_sem=ssem, recv_sem=rsem,
            device_id=to, device_id_type=pl.DeviceIdType.MESH,
        )

    C, Y, Z = 1, 2, 2 * B
    partner = at(C)
    barrier = pltpu.get_barrier_semaphore()
    along_z = [Z * k for k in range(1, A)] + ([Z + Y] if crossed else [])

    def signal(sem, to):
        pl.semaphore_signal(sem, inc=1, device_id=to, device_id_type=pl.DeviceIdType.MESH)

    def higher(mask):
        top = 1
        while 2 * top <= mask // Z:
            top *= 2
        return lax.rem(a // top, 2)

    for mask in [Y * k for k in range(1, B)] + [C]:
        signal(barrier, at(mask))
    for mask in along_z:
        @pl.when(higher(mask) == 0)
        def _():
            signal(barrier, at(mask))
    loads = [
        pltpu.make_async_copy(src, dst, load.at[k])
        for k, (src, dst) in enumerate(
            [(idx_hbm, idx_ref), (c_hbm, c_ref), (m_hbm, m_ref), (coef_hbm, coef_ref)]
        )
    ]
    for item in loads:
        item.start()
    pl.semaphore_wait(barrier, B + sum(higher(mask) for mask in along_z))

    sends = []

    def piece(ref, h):
        return ref.at[pl.ds(cuts[h][0], cuts[h][1])]

    for h in range(H):
        for k in range(1, B):
            sends.append(copy(
                piece(c_hbm, h), piece(cent.at[2 * k], h), cs_send.at[k * H + h],
                c_recv.at[2 * k * H + h], at(Y * k),
            ))
        if h == 0:
            for k in range(1, B):
                sends.append(
                    copy(coef_hbm, cfs.at[2 * k], cf_send.at[k], cf_recv.at[2 * k], at(Y * k))
                )
    sends.append(copy(coef_hbm, cfs.at[1], cf_send.at[0], cf_recv.at[1], partner))
    sends.append(copy(c_hbm, cent.at[1], cs_send.at[0], c_recv.at[H], partner))
    for s in sends:
        s.start()
    for i, mask in enumerate(along_z):
        @pl.when(higher(mask) == 1)
        def _():
            signal(z_here.at[i], at(mask))

    diag = lax.broadcasted_iota(jnp.int32, (rows, rows), 0) == lax.broadcasted_iota(
        jnp.int32, (rows, rows), 1
    )
    loads[0].wait()
    loads[1].wait()
    local_idx = (idx_ref[...] - me * own).astype(F32)
    column = jnp.sum(
        jnp.where(diag, jnp.broadcast_to(local_idx, (rows, rows)), 0.0), axis=1, keepdims=True
    )
    places = lax.broadcasted_iota(jnp.int32, (rows, own), 1).astype(F32)
    pick = jnp.where(places == column, 1.0, 0.0).astype(BF16)
    picked = jnp.dot(pick, c_ref[...], preferred_element_type=F32).astype(BF16)
    loads[2].wait()
    ucol[0] = jnp.dot(picked, m_ref[...], preferred_element_type=F32).astype(BF16)
    to_row = [
        copy(ucol.at[0], ucol.at[k], u_send.at[k], u_recv.at[k], at(Z * k)) for k in range(1, A)
    ]
    sends += to_row
    for i, mask in reversed(list(enumerate(along_z[: A - 1]))):
        @pl.when(higher(mask) == 1)
        def _():
            to_row[i].start()

    def coords(block):
        return jnp.dot(block, m_ref[...], preferred_element_type=F32).astype(BF16)

    def arrived(dst, rsem):
        copy(dst, dst, rsem, rsem, partner).wait_recv()

    def relay(k, h):
        j = 2 * k
        arrived(piece(cent.at[j], h), c_recv.at[j * H + h])
        first, count = cuts[h]
        cent[j, first : first + count] = coords(cent[j, first : first + count])
        hop = copy(
            piece(cent.at[j], h), piece(cent.at[j + 1], h),
            cs_send.at[(B - 1 + k) * H + h], c_recv.at[(j + 1) * H + h], partner,
        )
        hop.start()
        hops = [hop]
        if h == 0:
            arrived(cfs.at[j], cf_recv.at[j])
            hop = copy(
                cfs.at[j], cfs.at[j + 1], cf_send.at[B - 1 + k], cf_recv.at[j + 1], partner
            )
            hop.start()
            hops.append(hop)
        return hops

    def squared(v):
        vf = v.astype(F32)
        high, low = split(vf * vf)
        ones = jnp.ones((16, width), BF16)
        sums = lax.dot_general(ones, high, NT, preferred_element_type=F32) + lax.dot_general(
            ones, low, NT, preferred_element_type=F32
        )
        return sums[0:1]

    def ready(slot, block):
        v = coords(block)
        cent[slot] = v
        svs[slot] = squared(v)

    ready(0, c_ref[...])

    for i, mask in enumerate(along_z):
        @pl.when(higher(mask) == 0)
        def _():
            pl.semaphore_wait(z_here.at[i], 1)
            if i < A - 1:
                to_row[i].start()

    arrived(cent.at[1], c_recv.at[H])
    ready(1, cent[1])
    early = relay(1, 0)
    for k in range(1, A):
        arrived(ucol.at[k], u_recv.at[k])
    uf = ucol[...].reshape(A * rows, width).astype(F32)
    su_ref[...] = jnp.sum(uf * uf, axis=1, keepdims=True)
    acc[...] = jnp.zeros_like(acc)
    wsum[...] = jnp.zeros_like(wsum)

    def add_block(v, coef_row, sv):
        u = ucol[...].reshape(A * rows, width)
        cross = lax.dot_general(u, v, NT, preferred_element_type=F32)
        dist_sq = jnp.maximum(su_ref[...] + sv - 2.0 * cross, 0.0)
        radius = jnp.sqrt(dist_sq / width + 1.0)
        weight = coef_row * jnp.exp(-radius / 4.0) / (4.0 * width * radius)
        acc[...] += jnp.dot(weight.astype(BF16), v, preferred_element_type=F32)
        wsum[...] += jnp.sum(weight, axis=1, keepdims=True)

    def add_pair(k, h):
        j = 2 * k
        if h == 0:
            arrived(cfs.at[j + 1], cf_recv.at[j + 1])
        arrived(piece(cent.at[j + 1], h), c_recv.at[(j + 1) * H + h])
        first, count = cuts[h]
        span = slice(first, first + count)
        v = jnp.concatenate([cent[j, span], cent[j + 1, span]], axis=0)
        coef_row = jnp.concatenate([cfs[j][:, span], cfs[j + 1][:, span]], axis=1)
        add_block(v, coef_row, squared(v))

    loads[3].wait()
    arrived(cfs.at[1], cf_recv.at[1])
    add_block(
        cent[0:2].reshape(2 * own, width),
        jnp.concatenate([coef_ref[...], cfs[1]], axis=1),
        jnp.concatenate([svs[0], svs[1]], axis=1),
    )

    def row_step(k, hops):
        for h in range(1, H):
            hops = hops + relay(k, h)
            add_pair(k, h - 1)
        add_pair(k, H - 1)
        return hops

    sends += row_step(1, early)

    def later_step(k, _):
        for hop in row_step(k, relay(k, 0)):
            hop.wait_send()
        return 0

    if B > 2:
        lax.fori_loop(2, B, later_step, 0)

    S = halves(rows)
    short = rows // S

    def settled(k, part):
        first = k * rows + part * short
        u = ucol[k, part * short : (part + 1) * short].astype(F32)
        return acc[first : first + short] - wsum[first : first + short] * u

    for part in range(S):
        span = pl.ds(part * short, short)
        for k in [*range(2, A), 1]:
            psend[k, span] = settled(k, part).astype(BF16)
            s = copy(
                psend.at[k, span], precv.at[k, span], p_send.at[k * S + part],
                p_recv.at[k * S + part], at(Z * k),
            )
            s.start()
            sends.append(s)

    count = [0]

    def pass_on(part, slot, *masks):
        for mask in masks:
            s = copy(
                gall.at[part, slot], gall.at[part, slot ^ mask], g_send.at[count[0]],
                g_recv.at[part * n + (slot ^ mask)], at(mask),
            )
            count[0] += 1
            s.start()
            sends.append(s)

    def came(part, *slots):
        for slot in slots:
            arrived(gall.at[part, slot], g_recv.at[part * n + slot])

    def relayed(part, *slots):
        for slot in slots:
            came(part, slot)
            pass_on(part, slot, C)

    n = 2 * A * B
    samples = n * rows
    metric_rows = metric_ref.shape[0]
    padded = -(-metric_rows // 16) * 16
    own_grads = []
    for part in range(S):
        span = pl.ds(part * short, short)
        total = settled(0, part)
        for k in range(1, A):
            arrived(precv.at[k, span], p_recv.at[k * S + part])
            total += precv[k, span].astype(F32)
        high, low = split(total)
        both = lax.dot_general(
            jnp.concatenate([high, low], axis=0), m_ref[...], NT, preferred_element_type=F32
        )
        own_grads.append(both[:short] + both[short:])
        gall[part, 0] = own_grads[part].astype(BF16)
        if crossed:
            pass_on(part, 0, 2 * Z, Y, Z, Z + Y, C)
        else:
            pass_on(part, 0, *[Z * k for k in range(1, A)], *[Y * q for q in range(1, B)], C)

    grads = jnp.concatenate(own_grads, axis=0)
    largest = jnp.max(jnp.max(jnp.abs(grads), axis=1, keepdims=True), axis=0, keepdims=True)
    size = jnp.where(largest > 0.0, largest, 1.0) * 64.0
    line = lax.broadcasted_iota(jnp.int32, (padded, width), 0) + me * metric_rows
    choose = jnp.where(
        line == lax.broadcasted_iota(jnp.int32, (padded, width), 1), 1.0, 0.0
    ).astype(BF16)
    ghigh, glow = split(grads / size)
    left = jnp.concatenate([choose, ghigh, glow], axis=0)

    def gram(part, first, blocks):
        g = gall[part, first : first + blocks]
        full = g.reshape(blocks * short, width)
        inner = lax.dot_general(left, full, NT, preferred_element_type=F32)
        phigh, plow = split(inner[padded : padded + rows] + inner[padded + rows :])
        lhs = jnp.concatenate([inner[:padded].astype(BF16), phigh, plow], axis=0)
        gf = g.astype(F32)
        return [jnp.dot(lhs, full, preferred_element_type=F32), jnp.sum(gf * gf, axis=0)]

    grams = []
    if crossed:
        F = 2 * Z
        near = (Y, Z, Z + Y)
        for part in range(S):
            came(part, F)
            pass_on(part, F, Z + Y, Z, Y, C)
            relayed(part, *near)
        for part in range(S):
            came(part, C, *[slot + C for slot in near])
            grams.append(gram(part, 0, F))
            relayed(part, *[F + slot for slot in near])
        for part in range(S):
            came(part, F + C, *[F + slot + C for slot in near])
            grams.append(gram(part, F, F))
    else:
        for part in range(S):
            for k in range(A):
                if k:
                    came(part, Z * k)
                    pass_on(part, Z * k, *[Y * q for q in range(1, B)], C)
            for k in range(A):
                relayed(part, *[Z * k + Y * q for q in range(1, B)])
        for part in range(S):
            came(part, *range(C, n, 2))
            grams.append(gram(part, 0, n))

    result, squares = functools.reduce(lambda x, y: [x[0] + y[0], x[1] + y[1]], grams)
    trace = jnp.sum(
        jnp.sum(squares / samples, axis=1, keepdims=True), axis=0, keepdims=True
    )
    metric_ref[...] = (result[:metric_rows] / samples) * width / trace
    moved = result[padded : padded + rows] + result[padded + rows :]
    out_ref[...] = (moved / samples) * width / trace * size

    for s in sends:
        s.wait_send()


def finish(metric, moved, metric_ref, out_ref):
    metric_ref[...] = metric[...]
    out_ref[...] = moved[...]


def local(A, B, centres, sample_idx, coef, metric_factor):
    own, width = centres.shape
    rows = sample_idx.shape[0]
    n = A * B * 2
    dma = lambda k: pltpu.SemaphoreType.DMA((k,))
    vmem = pl.BlockSpec(memory_space=pltpu.VMEM)
    H = len(parts(own))
    S = halves(rows)
    limit = 60 * 2**20
    hbm = pl.BlockSpec(memory_space=pltpu.HBM)
    shapes = ((width // n, width), (rows, width))
    held = pl.pallas_call(
        functools.partial(kernel, A, B),
        out_shape=tuple(pltpu.VMEM(shape, F32) for shape in shapes),
        in_specs=[hbm] * 4,
        out_specs=(vmem, vmem),
        scratch_shapes=[
            pltpu.VMEM((own, width), BF16),
            pltpu.VMEM((1, rows), jnp.int32),
            pltpu.VMEM((1, own), F32),
            pltpu.VMEM((width, width), BF16),
            pltpu.VMEM((2 * B, own, width), BF16),
            pltpu.VMEM((2 * B, 1, own), F32),
            pltpu.VMEM((2 * B, 1, own), F32),
            pltpu.VMEM((A, rows, width), BF16),
            pltpu.VMEM((A * rows, width), F32),
            pltpu.VMEM((A * rows, 1), F32),
            pltpu.VMEM((A * rows, 1), F32),
            pltpu.VMEM((A, rows, width), BF16),
            pltpu.VMEM((A, rows, width), BF16),
            pltpu.VMEM((S, n, rows // S, width), BF16),
            dma(2 * B * H), dma(2 * B), dma(2 * B * H), dma(2 * B),
            dma(A), dma(A), dma(A * S), dma(A * S),
            dma((n + 16) * S), dma(n * S), dma(4),
            pltpu.SemaphoreType.REGULAR((A,)),
        ],
        compiler_params=pltpu.CompilerParams(
            collective_id=0, has_side_effects=True, vmem_limit_bytes=limit
        ),
    )(centres, sample_idx.reshape(1, rows), coef.reshape(1, own), metric_factor)
    return pl.pallas_call(
        finish,
        out_shape=tuple(jax.ShapeDtypeStruct(shape, F32) for shape in shapes),
        in_specs=[vmem] * 2,
        out_specs=(vmem, vmem),
        compiler_params=pltpu.CompilerParams(vmem_limit_bytes=40 * 2**20),
    )(*held)


def solution(mesh):
    chips = mesh.shape["ctr"] // 2
    A = 1
    while A * A < chips:
        A *= 2
    B = chips // A
    placed = (P(("grp", "ctr"), None), P(("grp", "ctr")), P(("grp", "ctr")), P())
    return jax.shard_map(
        functools.partial(local, A, B),
        mesh=mesh,
        in_specs=placed,
        out_specs=(P(("grp", "ctr"), None), P(("grp", "ctr"), None)),
        check_vma=False,
    )
```

```python
import functools

import jax
import jax.numpy as jnp
from jax import lax
from jax.experimental import pallas as pl
from jax.experimental.pallas import tpu as pltpu
from jax.sharding import PartitionSpec as P

F32 = jnp.float32
BF16 = jnp.bfloat16
NT = (((1,), (1,)), ((), ()))


def halves(rows):
    return 2 if rows % 32 == 0 else 1


def parts(own):
    first = own * 5 // 12 // 16 * 16
    return [(0, first), (first, own - first)]


def split(x):
    high = x.astype(BF16)
    return high, (x - high.astype(F32)).astype(BF16)


def flip(i, mask):
    out = i
    bit = 1
    while bit <= mask:
        if mask & bit:
            out = out + bit - 2 * bit * lax.rem(i // bit, 2)
        bit *= 2
    return out


def kernel(
    A, B, c_hbm, idx_hbm, coef_hbm, m_hbm, metric_ref, out_ref,
    c_ref, idx_ref, coef_ref, m_ref,
    cent, cfs, svs, ucol, acc, su_ref, wsum, psend, precv, gall,
    cs_send, cf_send, c_recv, cf_recv, u_send, u_recv, p_send, p_recv,
    g_send, g_recv, load, z_here,
):
    own, width = c_ref.shape
    rows = idx_ref.shape[1]
    cuts = parts(own)
    H = len(cuts)
    me = lax.axis_index("ctr")
    c = lax.rem(me, 2)
    b = lax.rem(me // 2, B)
    a = me // (2 * B)
    crossed = A == 4 and B == 2

    def dev(a_, b_, c_):
        return {"ctr": (a_ * B + b_) * 2 + c_}

    def at(mask):
        return {"ctr": flip(me, mask)}

    def copy(src, dst, ssem, rsem, to):
        return pltpu.make_async_remote_copy(
            src_ref=src, dst_ref=dst, send_sem=ssem, recv_sem=rsem,
            device_id=to, device_id_type=pl.DeviceIdType.MESH,
        )

    C, Y, Z = 1, 2, 2 * B
    partner = at(C)
    barrier = pltpu.get_barrier_semaphore()
    along_z = [Z * k for k in range(1, A)] + ([Z + Y] if crossed else [])

    def signal(sem, to):
        pl.semaphore_signal(sem, inc=1, device_id=to, device_id_type=pl.DeviceIdType.MESH)

    def higher(mask):
        top = 1
        while 2 * top <= mask // Z:
            top *= 2
        return lax.rem(a // top, 2)

    for mask in [Y * k for k in range(1, B)] + [C]:
        signal(barrier, at(mask))
    for mask in along_z:
        @pl.when(higher(mask) == 0)
        def _():
            signal(barrier, at(mask))
    loads = [
        pltpu.make_async_copy(src, dst, load.at[k])
        for k, (src, dst) in enumerate(
            [(idx_hbm, idx_ref), (c_hbm, c_ref), (m_hbm, m_ref), (coef_hbm, coef_ref)]
        )
    ]
    for item in loads:
        item.start()
    pl.semaphore_wait(barrier, B + sum(higher(mask) for mask in along_z))

    sends = []

    def piece(ref, h):
        return ref.at[pl.ds(cuts[h][0], cuts[h][1])]

    for h in range(H):
        for k in range(1, B):
            sends.append(copy(
                piece(c_hbm, h), piece(cent.at[2 * k], h), cs_send.at[k * H + h],
                c_recv.at[2 * k * H + h], at(Y * k),
            ))
        if h == 0:
            for k in range(1, B):
                sends.append(
                    copy(coef_hbm, cfs.at[2 * k], cf_send.at[k], cf_recv.at[2 * k], at(Y * k))
                )
    sends.append(copy(coef_hbm, cfs.at[1], cf_send.at[0], cf_recv.at[1], partner))
    sends.append(copy(c_hbm, cent.at[1], cs_send.at[0], c_recv.at[H], partner))
    for s in sends:
        s.start()
    for i, mask in enumerate(along_z):
        @pl.when(higher(mask) == 1)
        def _():
            signal(z_here.at[i], at(mask))

    diag = lax.broadcasted_iota(jnp.int32, (rows, rows), 0) == lax.broadcasted_iota(
        jnp.int32, (rows, rows), 1
    )
    loads[0].wait()
    loads[1].wait()
    local_idx = (idx_ref[...] - me * own).astype(F32)
    column = jnp.sum(
        jnp.where(diag, jnp.broadcast_to(local_idx, (rows, rows)), 0.0), axis=1, keepdims=True
    )
    places = lax.broadcasted_iota(jnp.int32, (rows, own), 1).astype(F32)
    pick = jnp.where(places == column, 1.0, 0.0).astype(BF16)
    picked = jnp.dot(pick, c_ref[...], preferred_element_type=F32).astype(BF16)
    loads[2].wait()
    ucol[0] = jnp.dot(picked, m_ref[...], preferred_element_type=F32).astype(BF16)
    to_row = [
        copy(ucol.at[0], ucol.at[k], u_send.at[k], u_recv.at[k], at(Z * k)) for k in range(1, A)
    ]
    sends += to_row
    for i, mask in reversed(list(enumerate(along_z[: A - 1]))):
        @pl.when(higher(mask) == 1)
        def _():
            to_row[i].start()

    def coords(block):
        return jnp.dot(block, m_ref[...], preferred_element_type=F32).astype(BF16)

    def arrived(dst, rsem):
        copy(dst, dst, rsem, rsem, partner).wait_recv()

    def relay(k, h):
        j = 2 * k
        arrived(piece(cent.at[j], h), c_recv.at[j * H + h])
        first, count = cuts[h]
        cent[j, first : first + count] = coords(cent[j, first : first + count])
        hop = copy(
            piece(cent.at[j], h), piece(cent.at[j + 1], h),
            cs_send.at[(B - 1 + k) * H + h], c_recv.at[(j + 1) * H + h], partner,
        )
        hop.start()
        hops = [hop]
        if h == 0:
            arrived(cfs.at[j], cf_recv.at[j])
            hop = copy(
                cfs.at[j], cfs.at[j + 1], cf_send.at[B - 1 + k], cf_recv.at[j + 1], partner
            )
            hop.start()
            hops.append(hop)
        return hops

    def squared(v):
        vf = v.astype(F32)
        high, low = split(vf * vf)
        ones = jnp.ones((16, width), BF16)
        sums = lax.dot_general(ones, high, NT, preferred_element_type=F32) + lax.dot_general(
            ones, low, NT, preferred_element_type=F32
        )
        return sums[0:1]

    def ready(slot, block):
        v = coords(block)
        cent[slot] = v
        svs[slot] = squared(v)

    ready(0, c_ref[...])

    for i, mask in enumerate(along_z):
        @pl.when(higher(mask) == 0)
        def _():
            pl.semaphore_wait(z_here.at[i], 1)
            if i < A - 1:
                to_row[i].start()

    arrived(cent.at[1], c_recv.at[H])
    ready(1, cent[1])
    early = relay(1, 0)
    for k in range(1, A):
        arrived(ucol.at[k], u_recv.at[k])
    uf = ucol[...].reshape(A * rows, width).astype(F32)
    su_ref[...] = jnp.sum(uf * uf, axis=1, keepdims=True)
    acc[...] = jnp.zeros_like(acc)
    wsum[...] = jnp.zeros_like(wsum)

    def add_block(v, coef_row, sv):
        u = ucol[...].reshape(A * rows, width)
        cross = lax.dot_general(u, v, NT, preferred_element_type=F32)
        dist_sq = jnp.maximum(su_ref[...] + sv - 2.0 * cross, 0.0)
        radius = jnp.sqrt(dist_sq / width + 1.0)
        weight = coef_row * jnp.exp(-radius / 4.0) / (4.0 * width * radius)
        acc[...] += jnp.dot(weight.astype(BF16), v, preferred_element_type=F32)
        wsum[...] += jnp.sum(weight, axis=1, keepdims=True)

    def add_pair(k, h):
        j = 2 * k
        if h == 0:
            arrived(cfs.at[j + 1], cf_recv.at[j + 1])
        arrived(piece(cent.at[j + 1], h), c_recv.at[(j + 1) * H + h])
        first, count = cuts[h]
        span = slice(first, first + count)
        v = jnp.concatenate([cent[j, span], cent[j + 1, span]], axis=0)
        coef_row = jnp.concatenate([cfs[j][:, span], cfs[j + 1][:, span]], axis=1)
        add_block(v, coef_row, squared(v))

    loads[3].wait()
    arrived(cfs.at[1], cf_recv.at[1])
    add_block(
        cent[0:2].reshape(2 * own, width),
        jnp.concatenate([coef_ref[...], cfs[1]], axis=1),
        jnp.concatenate([svs[0], svs[1]], axis=1),
    )

    def row_step(k, hops):
        for h in range(1, H):
            hops = hops + relay(k, h)
            add_pair(k, h - 1)
        add_pair(k, H - 1)
        return hops

    sends += row_step(1, early)

    def later_step(k, _):
        for hop in row_step(k, relay(k, 0)):
            hop.wait_send()
        return 0

    if B > 2:
        lax.fori_loop(2, B, later_step, 0)

    S = halves(rows)
    short = rows // S

    def settled(k, part):
        first = k * rows + part * short
        u = ucol[k, part * short : (part + 1) * short].astype(F32)
        return acc[first : first + short] - wsum[first : first + short] * u

    for part in range(S):
        span = pl.ds(part * short, short)
        for k in [*range(2, A), 1]:
            psend[k, span] = settled(k, part).astype(BF16)
            s = copy(
                psend.at[k, span], precv.at[k, span], p_send.at[k * S + part],
                p_recv.at[k * S + part], at(Z * k),
            )
            s.start()
            sends.append(s)

    count = [0]

    def pass_on(part, slot, *masks):
        for mask in masks:
            s = copy(
                gall.at[part, slot], gall.at[part, slot ^ mask], g_send.at[count[0]],
                g_recv.at[part * n + (slot ^ mask)], at(mask),
            )
            count[0] += 1
            s.start()
            sends.append(s)

    def came(part, *slots):
        for slot in slots:
            arrived(gall.at[part, slot], g_recv.at[part * n + slot])

    def relayed(part, *slots):
        for slot in slots:
            came(part, slot)
            pass_on(part, slot, C)

    n = 2 * A * B
    samples = n * rows
    metric_rows = metric_ref.shape[0]
    padded = -(-metric_rows // 16) * 16
    own_grads = []
    for part in range(S):
        span = pl.ds(part * short, short)
        total = settled(0, part)
        for k in range(1, A):
            arrived(precv.at[k, span], p_recv.at[k * S + part])
            total += precv[k, span].astype(F32)
        high, low = split(total)
        both = lax.dot_general(
            jnp.concatenate([high, low], axis=0), m_ref[...], NT, preferred_element_type=F32
        )
        own_grads.append(both[:short] + both[short:])
        gall[part, 0] = own_grads[part].astype(BF16)
        if crossed:
            pass_on(part, 0, 2 * Z, Y, Z, Z + Y, C)
        else:
            pass_on(part, 0, *[Z * k for k in range(1, A)], *[Y * q for q in range(1, B)], C)

    grads = jnp.concatenate(own_grads, axis=0)
    largest = jnp.max(jnp.max(jnp.abs(grads), axis=1, keepdims=True), axis=0, keepdims=True)
    size = jnp.where(largest > 0.0, largest, 1.0) * 64.0
    line = lax.broadcasted_iota(jnp.int32, (padded, width), 0) + me * metric_rows
    choose = jnp.where(
        line == lax.broadcasted_iota(jnp.int32, (padded, width), 1), 1.0, 0.0
    ).astype(BF16)
    ghigh, glow = split(grads / size)
    left = jnp.concatenate([choose, ghigh, glow], axis=0)

    def gram(part, first, blocks):
        g = gall[part, first : first + blocks]
        full = g.reshape(blocks * short, width)
        inner = lax.dot_general(left, full, NT, preferred_element_type=F32)
        phigh, plow = split(inner[padded : padded + rows] + inner[padded + rows :])
        lhs = jnp.concatenate([inner[:padded].astype(BF16), phigh, plow], axis=0)
        gf = g.astype(F32)
        return [jnp.dot(lhs, full, preferred_element_type=F32), jnp.sum(gf * gf, axis=0)]

    grams = []
    if crossed:
        F = 2 * Z
        near = (Y, Z, Z + Y)
        for part in range(S):
            came(part, F)
            pass_on(part, F, Z + Y, Z, Y, C)
            relayed(part, *near)
        for part in range(S):
            came(part, C, *[slot + C for slot in near])
            grams.append(gram(part, 0, F))
            relayed(part, *[F + slot for slot in near])
        for part in range(S):
            came(part, F + C, *[F + slot + C for slot in near])
            grams.append(gram(part, F, F))
    else:
        for part in range(S):
            for k in range(A):
                if k:
                    came(part, Z * k)
                    pass_on(part, Z * k, *[Y * q for q in range(1, B)], C)
            for k in range(A):
                relayed(part, *[Z * k + Y * q for q in range(1, B)])
        for part in range(S):
            came(part, *range(C, n, 2))
            grams.append(gram(part, 0, n))

    result, squares = functools.reduce(lambda x, y: [x[0] + y[0], x[1] + y[1]], grams)
    trace = jnp.sum(
        jnp.sum(squares / samples, axis=1, keepdims=True), axis=0, keepdims=True
    )
    metric_ref[...] = (result[:metric_rows] / samples) * width / trace
    moved = result[padded : padded + rows] + result[padded + rows :]
    out_ref[...] = (moved / samples) * width / trace * size

    for s in sends:
        s.wait_send()


def finish(metric, moved, metric_ref, out_ref):
    metric_ref[...] = metric[...]
    out_ref[...] = moved[...]


def local(A, B, centres, sample_idx, coef, metric_factor):
    own, width = centres.shape
    rows = sample_idx.shape[0]
    n = A * B * 2
    dma = lambda k: pltpu.SemaphoreType.DMA((k,))
    vmem = pl.BlockSpec(memory_space=pltpu.VMEM)
    H = len(parts(own))
    S = halves(rows)
    limit = 60 * 2**20
    hbm = pl.BlockSpec(memory_space=pltpu.HBM)
    shapes = ((width // n, width), (rows, width))
    held = pl.pallas_call(
        functools.partial(kernel, A, B),
        out_shape=tuple(pltpu.VMEM(shape, F32) for shape in shapes),
        in_specs=[hbm] * 4,
        out_specs=(vmem, vmem),
        scratch_shapes=[
            pltpu.VMEM((own, width), BF16),
            pltpu.VMEM((1, rows), jnp.int32),
            pltpu.VMEM((1, own), F32),
            pltpu.VMEM((width, width), BF16),
            pltpu.VMEM((2 * B, own, width), BF16),
            pltpu.VMEM((2 * B, 1, own), F32),
            pltpu.VMEM((2 * B, 1, own), F32),
            pltpu.VMEM((A, rows, width), BF16),
            pltpu.VMEM((A * rows, width), F32),
            pltpu.VMEM((A * rows, 1), F32),
            pltpu.VMEM((A * rows, 1), F32),
            pltpu.VMEM((A, rows, width), BF16),
            pltpu.VMEM((A, rows, width), BF16),
            pltpu.VMEM((S, n, rows // S, width), BF16),
            dma(2 * B * H), dma(2 * B), dma(2 * B * H), dma(2 * B),
            dma(A), dma(A), dma(A * S), dma(A * S),
            dma((n + 16) * S), dma(n * S), dma(4),
            pltpu.SemaphoreType.REGULAR((A,)),
        ],
        compiler_params=pltpu.CompilerParams(
            collective_id=0, has_side_effects=True, vmem_limit_bytes=limit
        ),
    )(centres, sample_idx.reshape(1, rows), coef.reshape(1, own), metric_factor)
    return pl.pallas_call(
        finish,
        out_shape=tuple(jax.ShapeDtypeStruct(shape, F32) for shape in shapes),
        in_specs=[vmem] * 2,
        out_specs=(vmem, vmem),
        compiler_params=pltpu.CompilerParams(vmem_limit_bytes=40 * 2**20),
    )(*held)


def solution(mesh):
    chips = mesh.shape["ctr"] // 2
    A = 1
    while A * A < chips:
        A *= 2
    B = chips // A
    placed = (P(("grp", "ctr"), None), P(("grp", "ctr")), P(("grp", "ctr")), P())
    return jax.shard_map(
        functools.partial(local, A, B),
        mesh=mesh,
        in_specs=placed,
        out_specs=(P(("grp", "ctr"), None), P(("grp", "ctr"), None)),
        check_vma=False,
    )
```

```python
import functools

import jax
import jax.numpy as jnp
from jax import lax
from jax.experimental import pallas as pl
from jax.experimental.pallas import tpu as pltpu
from jax.sharding import PartitionSpec as P

F32 = jnp.float32
BF16 = jnp.bfloat16
NT = (((1,), (1,)), ((), ()))


def halves(rows):
    return 2 if rows % 32 == 0 else 1


def parts(own):
    first = own * 5 // 12 // 16 * 16
    return [(0, first), (first, own - first)]


def split(x):
    high = x.astype(BF16)
    return high, (x - high.astype(F32)).astype(BF16)


def flip(i, mask):
    out = i
    bit = 1
    while bit <= mask:
        if mask & bit:
            out = out + bit - 2 * bit * lax.rem(i // bit, 2)
        bit *= 2
    return out


def kernel(
    A, B, c_hbm, idx_hbm, coef_hbm, m_hbm, metric_ref, out_ref,
    c_ref, idx_ref, coef_ref, m_ref,
    cent, cfs, svs, ucol, acc, su_ref, wsum, psend, precv, gall,
    cs_send, cf_send, c_recv, cf_recv, u_send, u_recv, p_send, p_recv,
    g_send, g_recv, load, z_here,
):
    own, width = c_ref.shape
    rows = idx_ref.shape[1]
    cuts = parts(own)
    H = len(cuts)
    me = lax.axis_index("ctr")
    c = lax.rem(me, 2)
    b = lax.rem(me // 2, B)
    a = me // (2 * B)
    crossed = A == 4 and B == 2
    n = 2 * A * B

    def dev(a_, b_, c_):
        return {"ctr": (a_ * B + b_) * 2 + c_}

    def at(mask):
        return {"ctr": flip(me, mask)}

    def copy(src, dst, ssem, rsem, to):
        return pltpu.make_async_remote_copy(
            src_ref=src, dst_ref=dst, send_sem=ssem, recv_sem=rsem,
            device_id=to, device_id_type=pl.DeviceIdType.MESH,
        )

    C, Y, Z = 1, 2, 2 * B
    partner = at(C)
    barrier = pltpu.get_barrier_semaphore()
    along_z = [Z * k for k in range(1, A)] + ([Z + Y] if crossed else [])

    def signal(sem, to):
        pl.semaphore_signal(sem, inc=1, device_id=to, device_id_type=pl.DeviceIdType.MESH)

    def higher(mask):
        top = 1
        while 2 * top <= mask // Z:
            top *= 2
        return lax.rem(a // top, 2)

    for mask in [Y * k for k in range(1, B)] + [C]:
        signal(barrier, at(mask))
    for mask in along_z:
        @pl.when(higher(mask) == 0)
        def _():
            signal(barrier, at(mask))
    loads = [
        pltpu.make_async_copy(src, dst, load.at[k])
        for k, (src, dst) in enumerate(
            [(idx_hbm, idx_ref), (c_hbm, c_ref), (m_hbm, m_ref), (coef_hbm, coef_ref)]
        )
    ]
    for item in loads:
        item.start()
    pl.semaphore_wait(barrier, B + sum(higher(mask) for mask in along_z))

    sends = []

    def piece(ref, h):
        return ref.at[pl.ds(cuts[h][0], cuts[h][1])]

    for h in range(H):
        for k in range(1, B):
            sends.append(copy(
                piece(c_hbm, h), piece(cent.at[2 * k], h), cs_send.at[k * H + h],
                c_recv.at[2 * k * H + h], at(Y * k),
            ))
        if h == 0:
            for k in range(1, B):
                sends.append(
                    copy(coef_hbm, cfs.at[2 * k], cf_send.at[k], cf_recv.at[2 * k], at(Y * k))
                )
    sends.append(copy(coef_hbm, cfs.at[1], cf_send.at[0], cf_recv.at[1], partner))
    sends.append(copy(c_hbm, cent.at[1], cs_send.at[0], c_recv.at[H], partner))
    for s in sends:
        s.start()
    for i, mask in enumerate(along_z):
        @pl.when(higher(mask) == 1)
        def _():
            signal(z_here.at[i], at(mask))

    diag = lax.broadcasted_iota(jnp.int32, (rows, rows), 0) == lax.broadcasted_iota(
        jnp.int32, (rows, rows), 1
    )
    loads[0].wait()
    loads[1].wait()
    local_idx = (idx_ref[...] - me * own).astype(F32)
    column = jnp.sum(
        jnp.where(diag, jnp.broadcast_to(local_idx, (rows, rows)), 0.0), axis=1, keepdims=True
    )
    places = lax.broadcasted_iota(jnp.int32, (rows, own), 1).astype(F32)
    pick = jnp.where(places == column, 1.0, 0.0).astype(BF16)
    picked = jnp.dot(pick, c_ref[...], preferred_element_type=F32).astype(BF16)
    loads[2].wait()
    ucol[0] = jnp.dot(picked, m_ref[...], preferred_element_type=F32).astype(BF16)
    to_row = [
        copy(ucol.at[0], ucol.at[k], u_send.at[k], u_recv.at[k], at(Z * k)) for k in range(1, A)
    ]
    sends += to_row
    for i, mask in reversed(list(enumerate(along_z[: A - 1]))):
        @pl.when(higher(mask) == 1)
        def _():
            to_row[i].start()

    def coords(block):
        return jnp.dot(block, m_ref[...], preferred_element_type=F32).astype(BF16)

    def arrived(dst, rsem):
        copy(dst, dst, rsem, rsem, partner).wait_recv()

    def relay(k, h):
        j = 2 * k
        arrived(piece(cent.at[j], h), c_recv.at[j * H + h])
        first, count = cuts[h]
        cent[j, first : first + count] = coords(cent[j, first : first + count])
        hop = copy(
            piece(cent.at[j], h), piece(cent.at[j + 1], h),
            cs_send.at[(B - 1 + k) * H + h], c_recv.at[(j + 1) * H + h], partner,
        )
        hop.start()
        hops = [hop]
        if h == 0:
            arrived(cfs.at[j], cf_recv.at[j])
            hop = copy(
                cfs.at[j], cfs.at[j + 1], cf_send.at[B - 1 + k], cf_recv.at[j + 1], partner
            )
            hop.start()
            hops.append(hop)
        return hops

    def squared(v):
        vf = v.astype(F32)
        high, low = split(vf * vf)
        ones = jnp.ones((16, width), BF16)
        sums = lax.dot_general(ones, high, NT, preferred_element_type=F32) + lax.dot_general(
            ones, low, NT, preferred_element_type=F32
        )
        return sums[0:1]

    def ready(slot, block):
        v = coords(block)
        cent[slot] = v
        svs[slot] = squared(v)

    ready(0, c_ref[...])

    for i, mask in enumerate(along_z):
        @pl.when(higher(mask) == 0)
        def _():
            pl.semaphore_wait(z_here.at[i], 1)
            if i < A - 1:
                to_row[i].start()

    arrived(cent.at[1], c_recv.at[H])
    ready(1, cent[1])
    early = relay(1, 0)
    for k in range(1, A):
        arrived(ucol.at[k], u_recv.at[k])
    uf = ucol[...].reshape(A * rows, width).astype(F32)
    su_ref[...] = jnp.sum(uf * uf, axis=1, keepdims=True)
    acc[...] = jnp.zeros_like(acc)
    wsum[...] = jnp.zeros_like(wsum)

    def add_block(v, coef_row, sv):
        u = ucol[...].reshape(A * rows, width)
        cross = lax.dot_general(u, v, NT, preferred_element_type=F32)
        dist_sq = jnp.maximum(su_ref[...] + sv - 2.0 * cross, 0.0)
        radius = jnp.sqrt(dist_sq / width + 1.0)
        weight = coef_row * jnp.exp(-radius / 4.0) / (4.0 * width * radius)
        acc[...] += jnp.dot(weight.astype(BF16), v, preferred_element_type=F32)
        wsum[...] += jnp.sum(weight, axis=1, keepdims=True)

    def add_pair(k, h):
        j = 2 * k
        if h == 0:
            arrived(cfs.at[j + 1], cf_recv.at[j + 1])
        arrived(piece(cent.at[j + 1], h), c_recv.at[(j + 1) * H + h])
        first, count = cuts[h]
        span = slice(first, first + count)
        v = jnp.concatenate([cent[j, span], cent[j + 1, span]], axis=0)
        coef_row = jnp.concatenate([cfs[j][:, span], cfs[j + 1][:, span]], axis=1)
        add_block(v, coef_row, squared(v))

    loads[3].wait()
    arrived(cfs.at[1], cf_recv.at[1])
    add_block(
        cent[0:2].reshape(2 * own, width),
        jnp.concatenate([coef_ref[...], cfs[1]], axis=1),
        jnp.concatenate([svs[0], svs[1]], axis=1),
    )

    def row_step(k, hops):
        for h in range(1, H):
            hops = hops + relay(k, h)
            add_pair(k, h - 1)
        add_pair(k, H - 1)
        return hops

    sends += row_step(1, early)

    def later_step(k, _):
        for hop in row_step(k, relay(k, 0)):
            hop.wait_send()
        return 0

    if B > 2:
        lax.fori_loop(2, B, later_step, 0)

    S = halves(rows)
    short = rows // S

    def settled(k, part):
        first = k * rows + part * short
        u = ucol[k, part * short : (part + 1) * short].astype(F32)
        return acc[first : first + short] - wsum[first : first + short] * u

    for part in range(S):
        span = pl.ds(part * short, short)
        for k in [*range(2, A), 1]:
            psend[k, span] = settled(k, part).astype(BF16)
            s = copy(
                psend.at[k, span], precv.at[k, span], p_send.at[k * S + part],
                p_recv.at[k * S + part], at(Z * k),
            )
            s.start()
            sends.append(s)

    count = [0]

    def pass_on(part, slot, *masks):
        for mask in masks:
            t = slot ^ mask
            send(gall.at[part, pos(slot)], gall.at[part, pos(t)], part * n + pos(t), at(mask))

    def send(src, dst, index, to):
        s = copy(src, dst, g_send.at[count[0]], g_recv.at[index], to)
        count[0] += 1
        s.start()
        sends.append(s)

    def pos(slot):
        return slot // 2 + (slot % 2) * (n // 2)

    def came(part, *slots):
        for slot in slots:
            arrived(gall.at[part, pos(slot)], g_recv.at[part * n + pos(slot)])

    def relayed(part, *slots):
        for slot in slots:
            came(part, slot)
            pass_on(part, slot, C)

    def run(part, slots, core):
        first = pos(slots[0] + core)
        return gall.at[part, pl.ds(first, len(slots))], part * n + first

    def relayed_run(part, slots):
        came(part, *slots)
        src, _ = run(part, slots, 0)
        dst, index = run(part, slots, C)
        send(src, dst, index, partner)

    def came_run(part, slots):
        dst, index = run(part, slots, C)
        arrived(dst, g_recv.at[index])

    def flush(keep):
        while len(sends) > keep:
            sends.pop(0).wait_send()

    samples = n * rows
    metric_rows = metric_ref.shape[0]
    padded = -(-metric_rows // 16) * 16
    own_grads = []
    for part in range(S):
        span = pl.ds(part * short, short)
        total = settled(0, part)
        for k in range(1, A):
            arrived(precv.at[k, span], p_recv.at[k * S + part])
            total += precv[k, span].astype(F32)
        high, low = split(total)
        both = lax.dot_general(
            jnp.concatenate([high, low], axis=0), m_ref[...], NT, preferred_element_type=F32
        )
        own_grads.append(both[:short] + both[short:])
        gall[part, 0] = own_grads[part].astype(BF16)
        if crossed:
            pass_on(part, 0, 2 * Z, Z + Y, Y, Z, C)
        else:
            pass_on(part, 0, *[Z * k for k in range(1, A)], *[Y * q for q in range(1, B)], C)

    grads = jnp.concatenate(own_grads, axis=0)
    largest = jnp.max(jnp.max(jnp.abs(grads), axis=1, keepdims=True), axis=0, keepdims=True)
    size = jnp.where(largest > 0.0, largest, 1.0) * 64.0
    line = lax.broadcasted_iota(jnp.int32, (padded, width), 0) + me * metric_rows
    choose = jnp.where(
        line == lax.broadcasted_iota(jnp.int32, (padded, width), 1), 1.0, 0.0
    ).astype(BF16)
    ghigh, glow = split(grads / size)
    left = jnp.concatenate([choose, ghigh, glow], axis=0)

    def gram(part, first, blocks):
        half = n // 2
        g = jnp.concatenate(
            [gall[part, first : first + blocks], gall[part, half + first : half + first + blocks]],
            axis=0,
        )
        full = g.reshape(2 * blocks * short, width)
        inner = lax.dot_general(left, full, NT, preferred_element_type=F32)
        phigh, plow = split(inner[padded : padded + rows] + inner[padded + rows :])
        lhs = jnp.concatenate([inner[:padded].astype(BF16), phigh, plow], axis=0)
        gf = g.astype(F32)
        return [jnp.dot(lhs, full, preferred_element_type=F32), jnp.sum(gf * gf, axis=0)]

    grams = []
    if crossed:
        F = 2 * Z
        near = (Y, Z, Z + Y)
        beyond = (F + Y, F + Z, F + Z + Y)
        for part in range(S):
            came(part, F)
            pass_on(part, F, Z + Y, Z, Y, C)
            relayed_run(part, near)
        for part in range(S):
            came(part, C)
            came_run(part, near)
            grams.append(gram(part, 0, F // 2))
            relayed_run(part, beyond)
        flush(S)
        for part in range(S):
            came(part, F + C)
            came_run(part, beyond)
            grams.append(gram(part, F // 2, F // 2))
    else:
        for part in range(S):
            for k in range(A):
                if k:
                    came(part, Z * k)
                    pass_on(part, Z * k, *[Y * q for q in range(1, B)], C)
            for k in range(A):
                relayed(part, *[Z * k + Y * q for q in range(1, B)])
        for part in range(S):
            came(part, *range(C, n, 2))
            grams.append(gram(part, 0, n // 2))

    result, squares = functools.reduce(lambda x, y: [x[0] + y[0], x[1] + y[1]], grams)
    trace = jnp.sum(
        jnp.sum(squares / samples, axis=1, keepdims=True), axis=0, keepdims=True
    )
    metric_ref[...] = (result[:metric_rows] / samples) * width / trace
    moved = result[padded : padded + rows] + result[padded + rows :]
    out_ref[...] = (moved / samples) * width / trace * size

    flush(0)


def finish(metric, moved, metric_ref, out_ref):
    metric_ref[...] = metric[...]
    out_ref[...] = moved[...]


def local(A, B, centres, sample_idx, coef, metric_factor):
    own, width = centres.shape
    rows = sample_idx.shape[0]
    n = A * B * 2
    dma = lambda k: pltpu.SemaphoreType.DMA((k,))
    vmem = pl.BlockSpec(memory_space=pltpu.VMEM)
    H = len(parts(own))
    S = halves(rows)
    limit = 60 * 2**20
    hbm = pl.BlockSpec(memory_space=pltpu.HBM)
    shapes = ((width // n, width), (rows, width))
    held = pl.pallas_call(
        functools.partial(kernel, A, B),
        out_shape=tuple(pltpu.VMEM(shape, F32) for shape in shapes),
        in_specs=[hbm] * 4,
        out_specs=(vmem, vmem),
        scratch_shapes=[
            pltpu.VMEM((own, width), BF16),
            pltpu.VMEM((1, rows), jnp.int32),
            pltpu.VMEM((1, own), F32),
            pltpu.VMEM((width, width), BF16),
            pltpu.VMEM((2 * B, own, width), BF16),
            pltpu.VMEM((2 * B, 1, own), F32),
            pltpu.VMEM((2 * B, 1, own), F32),
            pltpu.VMEM((A, rows, width), BF16),
            pltpu.VMEM((A * rows, width), F32),
            pltpu.VMEM((A * rows, 1), F32),
            pltpu.VMEM((A * rows, 1), F32),
            pltpu.VMEM((A, rows, width), BF16),
            pltpu.VMEM((A, rows, width), BF16),
            pltpu.VMEM((S, n, rows // S, width), BF16),
            dma(2 * B * H), dma(2 * B), dma(2 * B * H), dma(2 * B),
            dma(A), dma(A), dma(A * S), dma(A * S),
            dma((n + 16) * S), dma(n * S), dma(4),
            pltpu.SemaphoreType.REGULAR((A,)),
        ],
        compiler_params=pltpu.CompilerParams(
            collective_id=0, has_side_effects=True, vmem_limit_bytes=limit
        ),
    )(centres, sample_idx.reshape(1, rows), coef.reshape(1, own), metric_factor)
    return pl.pallas_call(
        finish,
        out_shape=tuple(jax.ShapeDtypeStruct(shape, F32) for shape in shapes),
        in_specs=[vmem] * 2,
        out_specs=(vmem, vmem),
        compiler_params=pltpu.CompilerParams(vmem_limit_bytes=40 * 2**20),
    )(*held)


def solution(mesh):
    chips = mesh.shape["ctr"] // 2
    A = 1
    while A * A < chips:
        A *= 2
    B = chips // A
    placed = (P(("grp", "ctr"), None), P(("grp", "ctr")), P(("grp", "ctr")), P())
    return jax.shard_map(
        functools.partial(local, A, B),
        mesh=mesh,
        in_specs=placed,
        out_specs=(P(("grp", "ctr"), None), P(("grp", "ctr"), None)),
        check_vma=False,
    )
```

```python
import functools

import jax
import jax.numpy as jnp
from jax import lax
from jax.experimental import pallas as pl
from jax.experimental.pallas import tpu as pltpu
from jax.sharding import PartitionSpec as P

F32 = jnp.float32
BF16 = jnp.bfloat16
NT = (((1,), (1,)), ((), ()))


def halves(rows):
    return 2 if rows % 32 == 0 else 1


def parts(own):
    first = own * 5 // 12 // 16 * 16
    return [(0, first), (first, own - first)]


def split(x):
    high = x.astype(BF16)
    return high, (x - high.astype(F32)).astype(BF16)


def flip(i, mask):
    out = i
    bit = 1
    while bit <= mask:
        if mask & bit:
            out = out + bit - 2 * bit * lax.rem(i // bit, 2)
        bit *= 2
    return out


def kernel(
    A, B, c_hbm, idx_hbm, coef_hbm, m_hbm, metric_ref, out_ref,
    c_ref, idx_ref, coef_ref, m_ref,
    cent, cfs, svs, ucol, acc, su_ref, wsum, psend, precv, gall,
    cs_send, cf_send, c_recv, cf_recv, u_send, u_recv, p_send, p_recv,
    g_send, g_recv, load, z_here,
):
    own, width = c_ref.shape
    rows = idx_ref.shape[1]
    cuts = parts(own)
    H = len(cuts)
    me = lax.axis_index("ctr")
    c = lax.rem(me, 2)
    b = lax.rem(me // 2, B)
    a = me // (2 * B)
    crossed = A == 4 and B == 2

    def dev(a_, b_, c_):
        return {"ctr": (a_ * B + b_) * 2 + c_}

    def at(mask):
        return {"ctr": flip(me, mask)}

    def copy(src, dst, ssem, rsem, to):
        return pltpu.make_async_remote_copy(
            src_ref=src, dst_ref=dst, send_sem=ssem, recv_sem=rsem,
            device_id=to, device_id_type=pl.DeviceIdType.MESH,
        )

    C, Y, Z = 1, 2, 2 * B
    partner = at(C)
    barrier = pltpu.get_barrier_semaphore()
    along_z = [Z * k for k in range(1, A)] + ([Z + Y] if crossed else [])

    def signal(sem, to):
        pl.semaphore_signal(sem, inc=1, device_id=to, device_id_type=pl.DeviceIdType.MESH)

    def higher(mask):
        top = 1
        while 2 * top <= mask // Z:
            top *= 2
        return lax.rem(a // top, 2)

    for mask in [Y * k for k in range(1, B)] + [C]:
        signal(barrier, at(mask))
    for mask in along_z:
        @pl.when(higher(mask) == 0)
        def _():
            signal(barrier, at(mask))
    loads = [
        pltpu.make_async_copy(src, dst, load.at[k])
        for k, (src, dst) in enumerate(
            [(idx_hbm, idx_ref), (c_hbm, c_ref), (m_hbm, m_ref), (coef_hbm, coef_ref)]
        )
    ]
    for item in loads:
        item.start()
    pl.semaphore_wait(barrier, B + sum(higher(mask) for mask in along_z))

    sends = []

    def piece(ref, h):
        return ref.at[pl.ds(cuts[h][0], cuts[h][1])]

    for h in range(H):
        for k in range(1, B):
            sends.append(copy(
                piece(c_hbm, h), piece(cent.at[2 * k], h), cs_send.at[k * H + h],
                c_recv.at[2 * k * H + h], at(Y * k),
            ))
        if h == 0:
            for k in range(1, B):
                sends.append(
                    copy(coef_hbm, cfs.at[2 * k], cf_send.at[k], cf_recv.at[2 * k], at(Y * k))
                )
    sends.append(copy(coef_hbm, cfs.at[1], cf_send.at[0], cf_recv.at[1], partner))
    sends.append(copy(c_hbm, cent.at[1], cs_send.at[0], c_recv.at[H], partner))
    for s in sends:
        s.start()
    for i, mask in enumerate(along_z):
        @pl.when(higher(mask) == 1)
        def _():
            signal(z_here.at[i], at(mask))

    diag = lax.broadcasted_iota(jnp.int32, (rows, rows), 0) == lax.broadcasted_iota(
        jnp.int32, (rows, rows), 1
    )
    loads[0].wait()
    loads[1].wait()
    local_idx = (idx_ref[...] - me * own).astype(F32)
    column = jnp.sum(
        jnp.where(diag, jnp.broadcast_to(local_idx, (rows, rows)), 0.0), axis=1, keepdims=True
    )
    places = lax.broadcasted_iota(jnp.int32, (rows, own), 1).astype(F32)
    pick = jnp.where(places == column, 1.0, 0.0).astype(BF16)
    picked = jnp.dot(pick, c_ref[...], preferred_element_type=F32).astype(BF16)
    loads[2].wait()
    ucol[0] = jnp.dot(picked, m_ref[...], preferred_element_type=F32).astype(BF16)
    to_row = [
        copy(ucol.at[0], ucol.at[k], u_send.at[k], u_recv.at[k], at(Z * k)) for k in range(1, A)
    ]
    sends += to_row
    for i, mask in reversed(list(enumerate(along_z[: A - 1]))):
        @pl.when(higher(mask) == 1)
        def _():
            to_row[i].start()

    def coords(block):
        return jnp.dot(block, m_ref[...], preferred_element_type=F32).astype(BF16)

    def arrived(dst, rsem):
        copy(dst, dst, rsem, rsem, partner).wait_recv()

    def relay(k, h):
        j = 2 * k
        arrived(piece(cent.at[j], h), c_recv.at[j * H + h])
        first, count = cuts[h]
        cent[j, first : first + count] = coords(cent[j, first : first + count])
        hop = copy(
            piece(cent.at[j], h), piece(cent.at[j + 1], h),
            cs_send.at[(B - 1 + k) * H + h], c_recv.at[(j + 1) * H + h], partner,
        )
        hop.start()
        hops = [hop]
        if h == 0:
            arrived(cfs.at[j], cf_recv.at[j])
            hop = copy(
                cfs.at[j], cfs.at[j + 1], cf_send.at[B - 1 + k], cf_recv.at[j + 1], partner
            )
            hop.start()
            hops.append(hop)
        return hops

    def squared(v):
        vf = v.astype(F32)
        high, low = split(vf * vf)
        ones = jnp.ones((16, width), BF16)
        sums = lax.dot_general(ones, high, NT, preferred_element_type=F32) + lax.dot_general(
            ones, low, NT, preferred_element_type=F32
        )
        return sums[0:1]

    def ready(slot, block):
        v = coords(block)
        cent[slot] = v
        svs[slot] = squared(v)

    ready(0, c_ref[...])

    for i, mask in enumerate(along_z):
        @pl.when(higher(mask) == 0)
        def _():
            pl.semaphore_wait(z_here.at[i], 1)
            if i < A - 1:
                to_row[i].start()

    arrived(cent.at[1], c_recv.at[H])
    ready(1, cent[1])
    early = relay(1, 0)
    for k in range(1, A):
        arrived(ucol.at[k], u_recv.at[k])
    uf = ucol[...].reshape(A * rows, width).astype(F32)
    su_ref[...] = jnp.sum(uf * uf, axis=1, keepdims=True)
    acc[...] = jnp.zeros_like(acc)
    wsum[...] = jnp.zeros_like(wsum)

    def add_block(v, coef_row, sv):
        u = ucol[...].reshape(A * rows, width)
        cross = lax.dot_general(u, v, NT, preferred_element_type=F32)
        dist_sq = jnp.maximum(su_ref[...] + sv - 2.0 * cross, 0.0)
        radius = jnp.sqrt(dist_sq / width + 1.0)
        weight = coef_row * jnp.exp(-radius / 4.0) / (4.0 * width * radius)
        acc[...] += jnp.dot(weight.astype(BF16), v, preferred_element_type=F32)
        wsum[...] += jnp.sum(weight, axis=1, keepdims=True)

    def add_pair(k, h):
        j = 2 * k
        if h == 0:
            arrived(cfs.at[j + 1], cf_recv.at[j + 1])
        arrived(piece(cent.at[j + 1], h), c_recv.at[(j + 1) * H + h])
        first, count = cuts[h]
        span = slice(first, first + count)
        v = jnp.concatenate([cent[j, span], cent[j + 1, span]], axis=0)
        coef_row = jnp.concatenate([cfs[j][:, span], cfs[j + 1][:, span]], axis=1)
        add_block(v, coef_row, squared(v))

    loads[3].wait()
    arrived(cfs.at[1], cf_recv.at[1])
    add_block(
        cent[0:2].reshape(2 * own, width),
        jnp.concatenate([coef_ref[...], cfs[1]], axis=1),
        jnp.concatenate([svs[0], svs[1]], axis=1),
    )

    def row_step(k, hops):
        for h in range(1, H):
            hops = hops + relay(k, h)
            add_pair(k, h - 1)
        add_pair(k, H - 1)
        return hops

    sends += row_step(1, early)

    def later_step(k, _):
        for hop in row_step(k, relay(k, 0)):
            hop.wait_send()
        return 0

    if B > 2:
        lax.fori_loop(2, B, later_step, 0)

    S = halves(rows)
    short = rows // S

    def settled(k, part):
        first = k * rows + part * short
        u = ucol[k, part * short : (part + 1) * short].astype(F32)
        return acc[first : first + short] - wsum[first : first + short] * u

    for part in range(S):
        span = pl.ds(part * short, short)
        for k in [*range(2, A), 1]:
            psend[k, span] = settled(k, part).astype(BF16)
            s = copy(
                psend.at[k, span], precv.at[k, span], p_send.at[k * S + part],
                p_recv.at[k * S + part], at(Z * k),
            )
            s.start()
            sends.append(s)

    count = [0]

    def pass_on(part, slot, *masks):
        for mask in masks:
            s = copy(
                gall.at[part, slot], gall.at[part, slot ^ mask], g_send.at[count[0]],
                g_recv.at[part * n + (slot ^ mask)], at(mask),
            )
            count[0] += 1
            s.start()
            sends.append(s)

    def came(part, *slots):
        for slot in slots:
            arrived(gall.at[part, slot], g_recv.at[part * n + slot])

    def relayed(part, *slots):
        for slot in slots:
            came(part, slot)
            pass_on(part, slot, C)

    n = 2 * A * B
    samples = n * rows
    metric_rows = metric_ref.shape[0]
    padded = -(-metric_rows // 16) * 16
    own_grads = []
    for part in range(S):
        span = pl.ds(part * short, short)
        total = settled(0, part)
        for k in range(1, A):
            arrived(precv.at[k, span], p_recv.at[k * S + part])
            total += precv[k, span].astype(F32)
        high, low = split(total)
        both = lax.dot_general(
            jnp.concatenate([high, low], axis=0), m_ref[...], NT, preferred_element_type=F32
        )
        own_grads.append(both[:short] + both[short:])
        gall[part, 0] = own_grads[part].astype(BF16)
        if crossed:
            pass_on(part, 0, 2 * Z, Z + Y, Y, Z, C)
        else:
            pass_on(part, 0, *[Z * k for k in range(1, A)], *[Y * q for q in range(1, B)], C)

    grads = jnp.concatenate(own_grads, axis=0)
    largest = jnp.max(jnp.max(jnp.abs(grads), axis=1, keepdims=True), axis=0, keepdims=True)
    size = jnp.where(largest > 0.0, largest, 1.0) * 64.0
    line = lax.broadcasted_iota(jnp.int32, (padded, width), 0) + me * metric_rows
    choose = jnp.where(
        line == lax.broadcasted_iota(jnp.int32, (padded, width), 1), 1.0, 0.0
    ).astype(BF16)
    ghigh, glow = split(grads / size)
    left = jnp.concatenate([choose, ghigh, glow], axis=0)

    def gram(part, first, blocks):
        g = gall[part, first : first + blocks]
        full = g.reshape(blocks * short, width)
        inner = lax.dot_general(left, full, NT, preferred_element_type=F32)
        phigh, plow = split(inner[padded : padded + rows] + inner[padded + rows :])
        lhs = jnp.concatenate([inner[:padded].astype(BF16), phigh, plow], axis=0)
        gf = g.astype(F32)
        return [jnp.dot(lhs, full, preferred_element_type=F32), jnp.sum(gf * gf, axis=0)]

    grams = []
    if crossed:
        F = 2 * Z
        near = (Y, Z, Z + Y)
        for part in range(S):
            came(part, F)
            pass_on(part, F, Z + Y, Z, Y, C)
            relayed(part, *near)
        for part in range(S):
            came(part, C, *[slot + C for slot in near])
            grams.append(gram(part, 0, F))
            relayed(part, *[F + slot for slot in near])
        for part in range(S):
            came(part, F + C, *[F + slot + C for slot in near])
            grams.append(gram(part, F, F))
    else:
        for part in range(S):
            for k in range(A):
                if k:
                    came(part, Z * k)
                    pass_on(part, Z * k, *[Y * q for q in range(1, B)], C)
            for k in range(A):
                relayed(part, *[Z * k + Y * q for q in range(1, B)])
        for part in range(S):
            came(part, *range(C, n, 2))
            grams.append(gram(part, 0, n))

    result, squares = functools.reduce(lambda x, y: [x[0] + y[0], x[1] + y[1]], grams)
    trace = jnp.sum(
        jnp.sum(squares / samples, axis=1, keepdims=True), axis=0, keepdims=True
    )
    metric_ref[...] = (result[:metric_rows] / samples) * width / trace
    moved = result[padded : padded + rows] + result[padded + rows :]
    out_ref[...] = (moved / samples) * width / trace * size

    for s in sends:
        s.wait_send()


def finish(metric, moved, metric_ref, out_ref):
    metric_ref[...] = metric[...]
    out_ref[...] = moved[...]


def local(A, B, centres, sample_idx, coef, metric_factor):
    own, width = centres.shape
    rows = sample_idx.shape[0]
    n = A * B * 2
    dma = lambda k: pltpu.SemaphoreType.DMA((k,))
    vmem = pl.BlockSpec(memory_space=pltpu.VMEM)
    H = len(parts(own))
    S = halves(rows)
    limit = 60 * 2**20
    hbm = pl.BlockSpec(memory_space=pltpu.HBM)
    shapes = ((width // n, width), (rows, width))
    held = pl.pallas_call(
        functools.partial(kernel, A, B),
        out_shape=tuple(pltpu.VMEM(shape, F32) for shape in shapes),
        in_specs=[hbm] * 4,
        out_specs=(vmem, vmem),
        scratch_shapes=[
            pltpu.VMEM((own, width), BF16),
            pltpu.VMEM((1, rows), jnp.int32),
            pltpu.VMEM((1, own), F32),
            pltpu.VMEM((width, width), BF16),
            pltpu.VMEM((2 * B, own, width), BF16),
            pltpu.VMEM((2 * B, 1, own), F32),
            pltpu.VMEM((2 * B, 1, own), F32),
            pltpu.VMEM((A, rows, width), BF16),
            pltpu.VMEM((A * rows, width), F32),
            pltpu.VMEM((A * rows, 1), F32),
            pltpu.VMEM((A * rows, 1), F32),
            pltpu.VMEM((A, rows, width), BF16),
            pltpu.VMEM((A, rows, width), BF16),
            pltpu.VMEM((S, n, rows // S, width), BF16),
            dma(2 * B * H), dma(2 * B), dma(2 * B * H), dma(2 * B),
            dma(A), dma(A), dma(A * S), dma(A * S),
            dma((n + 16) * S), dma(n * S), dma(4),
            pltpu.SemaphoreType.REGULAR((A,)),
        ],
        compiler_params=pltpu.CompilerParams(
            collective_id=0, has_side_effects=True, vmem_limit_bytes=limit
        ),
    )(centres, sample_idx.reshape(1, rows), coef.reshape(1, own), metric_factor)
    return pl.pallas_call(
        finish,
        out_shape=tuple(jax.ShapeDtypeStruct(shape, F32) for shape in shapes),
        in_specs=[vmem] * 2,
        out_specs=(vmem, vmem),
        compiler_params=pltpu.CompilerParams(vmem_limit_bytes=40 * 2**20),
    )(*held)


def solution(mesh):
    chips = mesh.shape["ctr"] // 2
    A = 1
    while A * A < chips:
        A *= 2
    B = chips // A
    placed = (P(("grp", "ctr"), None), P(("grp", "ctr")), P(("grp", "ctr")), P())
    return jax.shard_map(
        functools.partial(local, A, B),
        mesh=mesh,
        in_specs=placed,
        out_specs=(P(("grp", "ctr"), None), P(("grp", "ctr"), None)),
        check_vma=False,
    )
```
